768 devices in a mesh: tile: 32 (over x, y_hi, core), kern: 24 (over z, y_lo).
Axes of the slice: x: 4, y: 8 (y_hi: 4, y_lo: 2; y = y_hi * 2 + y_lo), z: 12, core: 2. Of those that a mesh axis runs over, the one named last changes fastest.
Arguments:
- mask_pixels: bfloat16 [1152, 36864], P(None, 'tile'), may hold values from -6 to 6
- orientation: int32 [32, 2], P('tile'), may hold values 0 or 1
- target_pattern: int32 [1152, 36864], P('kern', 'tile'), may hold values 0 or 1
- kernel_real: float32 [24, 64, 64], P('kern'), may hold values from -6 to 6
- kernel_imag: float32 [24, 64, 64], P('kern'), may hold values from -6 to 6
- eigen_weights: float32 [24], P('kern'), may hold values from 0.01 to 0.1
Outputs:
- mask_gradient: float32 [1152, 36864], P('kern', 'tile')
The draws below stay inside these ranges and needn't reach their ends.
Inputs may be any that keep to these rules, and one draw needn't show every extreme that they name: `orientation`: 1 takes the neighbour's facing strip in order, 0 reversed; the entry for a side without neighbour is unused.
All inputs are finite; a program needn't handle non-finite values. No bound on the sum of `orientation` or of `target_pattern` on one device may be relied on, other than what follows from the above.
Results may differ from the reference program's by a relative error of at most 0.018.
Values may be sent and summed in bfloat16 or wider, within the bound.
A program may use at most 64 MiB of HBM per device.

```python
import math
import jax
import jax.numpy as jnp
from jax import lax

N = 1152
HALO = 64
KF = 64
KERNELS = 24
TILES = 32
NE = 1280


def touch_ends(drawn, rng, smallest, top_value):
    dims = drawn.shape
    place = [jax.random.randint(jax.random.fold_in(rng, axis), (), 0, dims[axis]) for axis in range(len(dims))]
    drawn = drawn.at[tuple(place)].set(smallest)
    longest = dims.index(max(dims))
    place[longest] = (place[longest] + 1) % dims[longest]
    return drawn.at[tuple(place)].set(top_value)


def block_scale(own_key, shape, shards, low, largest):
    def one(dim, parts):
        heights = jax.random.uniform(jax.random.fold_in(jax.random.fold_in(own_key, 6), dim), (parts,), jnp.float32, low / len(shards), largest / len(shards))
        return jnp.repeat(jnp.exp(heights), shape[dim] // parts).reshape((-1,) + (1,) * (len(shape) - dim - 1))

    factor_of = one(*shards[0])
    for cut in shards[1:]:
        factor_of = factor_of * one(*cut)
    return factor_of


def scatter_about(key, dims, deviation, most, shards=(), kind=jnp.bfloat16):
    drawn = jax.random.normal(key, dims, jnp.float32) * deviation
    if len(shards) > 0:
        drawn = block_scale(key, dims, shards, -0.22, 0.18) * drawn
    return jnp.clip(drawn, min=-most, max=most).astype(kind)


def setup_inputs(seed: int = 0) -> dict:
    key_list = jax.random.split(jax.random.key(seed), 7)
    mask_pixels = scatter_about(key_list[0], (N, TILES * N), 1.0, 6.0, ((1, 32),))
    orientation = touch_ends((jax.random.randint(key_list[1], (TILES, 2), 0, 2) < 1).astype(jnp.int32), jax.random.fold_in(key_list[1], 1), 0, 1)
    target_pattern = touch_ends((jax.random.randint(key_list[2], (N, TILES * N), 0, 2) < 1).astype(jnp.int32), jax.random.fold_in(key_list[2], 1), 0, 1)
    kernel_real = scatter_about(key_list[3], (KERNELS, KF, KF), 1.0, 6.0, ((0, 24),), jnp.float32)
    kernel_imag = scatter_about(key_list[4], (KERNELS, KF, KF), 1.0, 6.0, ((0, 24),), jnp.float32)
    eigen_weights = jnp.clip(jnp.exp(math.log(0.1) - 2.3025851 * jax.random.uniform(key_list[5], (KERNELS,), jnp.float32) ** block_scale(key_list[5], (KERNELS,), ((0, 24),), -0.2, 0.2)), 0.01, 0.1)
    return dict(mask_pixels=mask_pixels, orientation=orientation, target_pattern=target_pattern, kernel_real=kernel_real, kernel_imag=kernel_imag, eigen_weights=eigen_weights)


STEEPNESS = 4.0
THRESHOLD = 1.0


def wave_tables(first, length):
    position = first + lax.iota(jnp.int32, length)
    frequency = lax.iota(jnp.int32, KF) - KF // 2
    phase = jnp.mod(position[:, None] * frequency[None, :], NE).astype(jnp.float32) * (2.0 * math.pi / NE)
    return jnp.cos(phase).astype(jnp.bfloat16), jnp.sin(phase).astype(jnp.bfloat16)


def transform_tables():
    cos_full, sin_full = wave_tables(0, NE)
    cos_mid = cos_full[HALO:HALO + N]
    sin_mid = sin_full[HALO:HALO + N]
    full_pair = jnp.concatenate([cos_full, sin_full], 1)
    mid_pair = jnp.concatenate([cos_mid, sin_mid], 1)
    to_columns = jnp.concatenate([jnp.concatenate([cos_mid.T, sin_mid.T], 1), jnp.concatenate([-sin_mid.T, cos_mid.T], 1)], 0)
    from_columns = jnp.concatenate([jnp.concatenate([cos_mid, -sin_mid], 1), jnp.concatenate([sin_mid, cos_mid], 1)], 0)
    to_extended = jnp.concatenate([jnp.concatenate([cos_full.T, sin_full.T], 1), jnp.concatenate([-sin_full.T, cos_full.T], 1)], 0)
    return full_pair, mid_pair, to_columns, from_columns, to_extended


def mask_spectrum(row_spectrum, mid_pair):
    blocks = lax.dot_general(mid_pair, row_spectrum, (((0,), (0,)), ((), ())), preferred_element_type=jnp.float32)
    spec_real = blocks[:KF, :KF] - blocks[KF:, KF:]
    spec_imag = -(blocks[:KF, KF:] + blocks[KF:, :KF])
    return spec_real, spec_imag


def column_fields(kernel_re, kernel_im, spec_real, spec_imag, to_columns):
    scale = 1.0 / (NE * KF)
    product = jnp.concatenate([kernel_re * spec_real - kernel_im * spec_imag, kernel_re * spec_imag + kernel_im * spec_real], 1) * scale
    columns = jnp.dot(product.astype(jnp.bfloat16), to_columns, preferred_element_type=jnp.float32).astype(jnp.bfloat16)
    return jnp.concatenate([columns, jnp.concatenate([-columns[:, N:], columns[:, :N]], 1)], 0)


def intensity_term(fields, weight):
    field_real = fields[..., :N].astype(jnp.float32)
    field_imag = fields[..., N:].astype(jnp.float32)
    return weight * (field_real * field_real + field_imag * field_imag)


def resist_slope(intensity, target_rows):
    resist = jax.nn.sigmoid(STEEPNESS * (intensity - THRESHOLD))
    return (2.0 * (resist - target_rows.astype(jnp.float32)) * STEEPNESS * resist * (1.0 - resist)).astype(jnp.bfloat16)


def weighted_fields(fields, slope):
    doubled = jnp.concatenate([slope, slope], 1).astype(jnp.float32)
    return (fields.astype(jnp.float32) * doubled).astype(jnp.bfloat16)


def adjoint_spectrum(blocks, kernel_re, kernel_im, weight):
    wave_real = blocks[:KF, :KF] + blocks[KF:, KF:]
    wave_imag = blocks[:KF, KF:] - blocks[KF:, :KF]
    factor = 2.0 * weight / (NE * KF)
    return factor * (kernel_re * wave_real + kernel_im * wave_imag), factor * (kernel_re * wave_imag - kernel_im * wave_real)


def extended_gradient(grad_real, grad_imag, row_pair, to_extended):
    combined = jnp.concatenate([grad_real, grad_imag], 1).astype(jnp.bfloat16)
    waves = jnp.dot(combined, to_extended, preferred_element_type=jnp.float32).astype(jnp.bfloat16)
    stacked = jnp.concatenate([waves[:, :NE], -waves[:, NE:]], 0)
    return jnp.dot(row_pair, stacked, preferred_element_type=jnp.float32)


def reference(mask_pixels, orientation, target_pattern, kernel_real, kernel_imag, eigen_weights):
    full_pair, mid_pair, to_columns, from_columns, to_extended = transform_tables()
    padded = jnp.pad(mask_pixels, ((0, 0), (HALO, HALO)))

    def one_tile(tile_index):
        offset = (tile_index * N).astype(jnp.int32)
        extended = lax.dynamic_slice(padded, (jnp.int32(0), offset), (N, NE))
        flag_pair = orientation[tile_index]
        left_rim = extended[:, :HALO]
        right_rim = extended[:, HALO + N:]
        left_rim = jnp.where(flag_pair[0] == 1, left_rim, left_rim[:, ::-1])
        right_rim = jnp.where(flag_pair[1] == 1, right_rim, right_rim[:, ::-1])
        extended = jnp.concatenate([left_rim, extended[:, HALO:HALO + N], right_rim], 1)
        row_spectrum = jnp.dot(extended, full_pair, preferred_element_type=jnp.float32).astype(jnp.bfloat16)
        spec_real, spec_imag = mask_spectrum(row_spectrum, mid_pair)

        def forward(running, kernel):
            one_real, one_imag, weight = kernel
            stacked = column_fields(one_real, one_imag, spec_real, spec_imag, to_columns)
            fields = jnp.dot(mid_pair, stacked, preferred_element_type=jnp.float32).astype(jnp.bfloat16)
            term = intensity_term(fields, weight).astype(jnp.bfloat16)
            return running + term.astype(jnp.float32), fields

        intensity, all_fields = lax.scan(forward, jnp.zeros((N, N), jnp.float32), (kernel_real, kernel_imag, eigen_weights))
        target_tile = lax.dynamic_slice(target_pattern, (jnp.int32(0), offset), (N, N))
        slope = resist_slope(intensity, target_tile)

        def backward(running, kernel):
            one_real, one_imag, weight, fields = kernel
            weighted = weighted_fields(fields, slope)
            partial_rows = jnp.dot(weighted, from_columns, preferred_element_type=jnp.float32).astype(jnp.bfloat16)
            blocks = lax.dot_general(mid_pair, partial_rows, (((0,), (0,)), ((), ())), preferred_element_type=jnp.float32)
            add_real, add_imag = adjoint_spectrum(blocks, one_real, one_imag, weight)
            return (running[0] + add_real, running[1] + add_imag), None

        empty = jnp.zeros((KF, KF), jnp.float32)
        (grad_real, grad_imag), unused = lax.scan(backward, (empty, empty), (kernel_real, kernel_imag, eigen_weights, all_fields))
        return extended_gradient(grad_real, grad_imag, mid_pair, to_extended)

    tile_grads = lax.map(one_tile, jnp.arange(TILES, dtype=jnp.int32))
    flag_left = orientation[:, 0][:, None, None]
    flag_right = orientation[:, 1][:, None, None]
    left_send = tile_grads[:, :, :HALO]
    right_send = tile_grads[:, :, HALO + N:]
    left_send = jnp.where(flag_left == 1, left_send, left_send[:, :, ::-1])
    right_send = jnp.where(flag_right == 1, right_send, right_send[:, :, ::-1])
    nothing = jnp.zeros((1, N, HALO), jnp.float32)
    from_left = jnp.concatenate([nothing, right_send[:-1]], 0)
    from_right = jnp.concatenate([left_send[1:], nothing], 0)
    middle = jnp.zeros((TILES, N, N - 2 * HALO), jnp.float32)
    gradient = tile_grads[:, :, HALO:HALO + N] + jnp.concatenate([from_left, middle, from_right], 2)
    return jnp.transpose(gradient, (1, 0, 2)).reshape(N, TILES * N)
```

```python
import math

import jax
import jax.numpy as jnp
import ml_dtypes
import numpy as np
from jax import lax
from jax.experimental import pallas as pl
from jax.experimental.pallas import tpu as pltpu
from jax.sharding import PartitionSpec as P

N = 1152
HALO = 64
KF = 64
NE = 1280
LANES = 128
CHUNKS = N // LANES
GROUP = 4

STEEPNESS = 4.0
THRESHOLD = 1.0
F32 = jnp.float32
BF16 = jnp.bfloat16
MESH = pl.DeviceIdType.MESH


def wave_pair():
    phase = np.mod(np.arange(NE)[:, None] * (np.arange(KF) - KF // 2)[None, :], NE).astype(np.float32)
    phase = phase * np.float32(2.0 * math.pi / NE)
    return np.concatenate([np.cos(phase), np.sin(phase)], 1).astype(ml_dtypes.bfloat16)


def tables(ranks):
    full = wave_pair()
    mid = full[HALO : HALO + N]
    right, left = full[HALO + N :], full[:HALO]
    rim = np.stack([np.concatenate([right, left]), np.concatenate([right[::-1], left[::-1]])])
    rows_t = np.transpose(mid.reshape(ranks, N // ranks, 2 * KF), (0, 2, 1))
    return mid, mid.T.copy(), rows_t.copy(), rim, np.transpose(rim, (0, 2, 1)).copy()


def dot(a, b):
    return jnp.dot(a, b, preferred_element_type=F32)


def body(
    ranks,
    orient,
    weight,
    mask_hbm,
    target_hbm,
    hr_hbm,
    hi_hbm,
    mid_hbm,
    mid_t_hbm,
    rows_t_hbm,
    rim_ref,
    rim_t_ref,
    out_ref,
    mask,
    target,
    hr,
    hi,
    mid,
    mid_t,
    rows,
    rows_t,
    spec_all,
    part_all,
    strip,
    halo_low,
    halo_high,
    columns,
    stacked,
    lines,
    to_cols,
    from_cols,
    fields,
    partial,
    margin,
    margin_low,
    margin_high,
    local_sem,
    spec_send,
    spec_recv,
    part_send,
    part_recv,
    tile_send,
    tile_recv,
):
    tiles = lax.axis_size("tile")
    tile = lax.axis_index("tile")
    rank = lax.axis_index("kern")
    up = lax.rem(tile + 1, tiles)
    down = lax.rem(tile + tiles - 1, tiles)
    count = N // ranks

    def load(src, dst, slot):
        copy = pltpu.make_async_copy(src, dst, local_sem.at[slot])
        copy.start()
        return copy

    barrier = pltpu.get_barrier_semaphore()
    for step in range(1, ranks):
        pl.semaphore_signal(
            barrier, inc=1, device_id={"kern": lax.rem(rank + step, ranks)}, device_id_type=MESH
        )
    for other in (up, down):
        pl.semaphore_signal(barrier, inc=1, device_id={"tile": other}, device_id_type=MESH)

    get_hr = load(hr_hbm.at[0], hr, 0)
    get_hi = load(hi_hbm.at[0], hi, 1)
    get_mid_t = load(mid_t_hbm, mid_t, 2)
    get_first = load(mask_hbm.at[:, 0:LANES], mask.at[:, 0:LANES], 3)
    get_last = load(mask_hbm.at[:, N - LANES : N], mask.at[:, N - LANES : N], 4)
    get_inner = load(mask_hbm.at[:, LANES : N - LANES], mask.at[:, LANES : N - LANES], 5)
    get_mid = load(mid_hbm, mid, 6)
    get_rows = load(mid_hbm.at[pl.ds(pl.multiple_of(rank * count, 16), count)], rows, 7)
    get_rows_t = load(rows_t_hbm.at[rank], rows_t, 8)
    get_target = load(target_hbm, target, 9)

    low = lax.broadcasted_iota(jnp.int32, (KF, 2 * KF), 1) < KF
    plus = jnp.where(low, 1.0, -1.0)
    minus = -plus

    def swap(x):
        return pltpu.roll(x, KF, 1)

    get_hr.wait()
    get_hi.wait()
    root = jnp.sqrt(jnp.full((KF, 2 * KF), weight[0], F32))
    spec_all[rank] = (jnp.concatenate([hr[...], hi[...]], 1) * root).astype(BF16)

    pl.semaphore_wait(barrier, ranks + 1)

    spec_copies = []
    for step in range(1, ranks):
        copy = pltpu.make_async_remote_copy(
            src_ref=spec_all.at[rank],
            dst_ref=spec_all.at[rank],
            send_sem=spec_send.at[step],
            recv_sem=spec_recv.at[step],
            device_id={"kern": lax.rem(rank + step, ranks)},
            device_id_type=MESH,
        )
        copy.start()
        spec_copies.append(copy)

    def to_neighbours(src, dst_up, dst_down, first):
        copies = []
        for place, (dst, other) in enumerate(((dst_up, up), (dst_down, down))):
            copy = pltpu.make_async_remote_copy(
                src_ref=src,
                dst_ref=dst,
                send_sem=tile_send.at[first + place],
                recv_sem=tile_recv.at[first + place],
                device_id={"tile": other},
                device_id_type=MESH,
            )
            copy.start()
            copies.append(copy)
        return copies

    get_mid_t.wait()
    get_first.wait()
    get_last.wait()
    first = dot(mid_t[...], mask[:, 0:LANES]).astype(BF16)
    last = dot(mid_t[...], mask[:, N - LANES : N]).astype(BF16)
    columns[:, 0:LANES] = first
    columns[:, N - LANES : N] = last
    edge = lax.broadcasted_iota(jnp.int32, (2 * KF, LANES), 1) < HALO
    strip[...] = jnp.where(edge, first.astype(F32), last.astype(F32)).astype(BF16)
    halo_copies = to_neighbours(strip, halo_low, halo_high, 0)

    get_inner.wait()
    for j in range(1, CHUNKS - 1):
        columns[:, j * LANES : (j + 1) * LANES] = dot(
            mid_t[...], mask[:, j * LANES : (j + 1) * LANES]
        ).astype(BF16)

    get_mid.wait()
    wide = lax.broadcasted_iota(jnp.int32, (LANES, 2 * KF), 1) < KF
    for j in range(CHUNKS):
        part = mid_t[:, j * LANES : (j + 1) * LANES]
        to_cols[j, 0:KF, 0:LANES] = part[:KF]
        to_cols[j, 0:KF, LANES:] = part[KF:]
        to_cols[j, KF:, 0:LANES] = -part[KF:]
        to_cols[j, KF:, LANES:] = part[:KF]
        block = mid[j * LANES : (j + 1) * LANES].astype(F32)
        from_cols[j, 0:LANES] = jnp.where(wide, block, -block).astype(BF16)
        from_cols[j, LANES:] = swap(block).astype(BF16)

    keep_right = orient[0, 1].astype(F32)
    keep_left = orient[0, 0].astype(F32)

    blocks = dot(columns[...], mid[...])
    upper = lax.broadcasted_iota(jnp.int32, (LANES, LANES), 0) < HALO
    keep = jnp.where(upper, keep_right, keep_left)
    rim = keep * rim_ref[0].astype(F32) + (1.0 - keep) * rim_ref[1].astype(F32)
    there = jnp.where(upper, jnp.where(tile < tiles - 1, 1.0, 0.0), jnp.where(tile > 0, 1.0, 0.0))
    rim = (rim * there).astype(BF16)
    for copy in halo_copies:
        copy.wait_recv()
    halo = jnp.where(edge, halo_high[...].astype(F32), halo_low[...].astype(F32)).astype(BF16)
    blocks = blocks + dot(halo, rim)
    lower = swap(blocks[KF:])
    spec = jnp.where(low, blocks[:KF] - lower, -(blocks[:KF] + lower)) * (1.0 / (NE * KF))
    spec_turned = swap(spec) * minus

    def kernel_parts(k):
        both = spec_all[k].astype(F32)
        other = swap(both)
        return jnp.where(low, both, other), jnp.where(low, other, both)

    get_rows.wait()
    for copy in spec_copies:
        copy.wait_recv()
    for k in range(ranks):
        real, imag = kernel_parts(k)
        product = real * spec + imag * spec_turned
        stacked[0:KF, k * LANES : (k + 1) * LANES] = product.astype(BF16)
        stacked[KF:, k * LANES : (k + 1) * LANES] = (swap(product) * minus).astype(BF16)
    for k in range(0, ranks, 2):
        pair = dot(rows[...], stacked[:, k * LANES : (k + 2) * LANES]).astype(BF16)
        lines[k * count : (k + 1) * count] = pair[:, :LANES]
        lines[(k + 1) * count : (k + 2) * count] = pair[:, LANES:]
    partial[...] = jnp.zeros_like(partial)
    get_target.wait()

    size = GROUP * count

    def chunk(j, carry):
        total = jnp.zeros((count, LANES), F32)
        for b in range(ranks // GROUP):
            field = dot(lines[b * size : (b + 1) * size], to_cols[j])
            for i in range(GROUP):
                one = field[i * count : (i + 1) * count]
                total = total + (one[:, :LANES] * one[:, :LANES] + one[:, LANES:] * one[:, LANES:])
            fields[b * size : (b + 1) * size] = field.astype(BF16)
        wanted = target[:, pl.ds(pl.multiple_of(j * LANES, LANES), LANES)].astype(F32)
        resist = 1.0 / (1.0 + jnp.exp(-STEEPNESS * (total - THRESHOLD)))
        slope = (2.0 * (resist - wanted) * STEEPNESS * resist * (1.0 - resist)).astype(BF16)
        slope = jnp.concatenate([slope, slope], 1)
        slope = jnp.concatenate([slope] * GROUP, 0)
        for b in range(ranks // GROUP):
            weighted = fields[b * size : (b + 1) * size] * slope
            partial[b * size : (b + 1) * size] += dot(weighted, from_cols[j])
        return carry

    lax.fori_loop(0, CHUNKS, chunk, 0)

    get_rows_t.wait()
    grad = jnp.zeros((KF, 2 * KF), F32)
    for k in range(0, ranks, 2):
        pair = jnp.concatenate(
            [
                partial[k * count : (k + 1) * count].astype(BF16),
                partial[(k + 1) * count : (k + 2) * count].astype(BF16),
            ],
            1,
        )
        wave = dot(rows_t[...], pair)
        for i in range(2):
            one = wave[:, i * LANES : (i + 1) * LANES]
            one = one[:KF] + swap(one[KF:]) * plus
            real, imag = kernel_parts(k + i)
            grad = grad + real * one + imag * (swap(one) * plus)
    part_all[rank] = (grad * (2.0 / (NE * KF))).astype(BF16)

    part_copies = []
    for step in range(1, ranks):
        copy = pltpu.make_async_remote_copy(
            src_ref=part_all.at[rank],
            dst_ref=part_all.at[rank],
            send_sem=part_send.at[step],
            recv_sem=part_recv.at[step],
            device_id={"kern": lax.rem(rank + step, ranks)},
            device_id_type=MESH,
        )
        copy.start()
        part_copies.append(copy)
    for copy in part_copies:
        copy.wait_recv()
    grad = jnp.zeros((KF, 2 * KF), F32)
    for k in range(ranks):
        grad = grad + part_all[k].astype(F32)
    grad = grad.astype(BF16).astype(F32)
    both = jnp.concatenate([grad, swap(grad) * minus], 0).astype(BF16)
    line = dot(rows[...], both)
    side = lax.broadcasted_iota(jnp.int32, (count, 2 * KF), 1) < KF
    line = jnp.where(side, line, -line).astype(BF16)
    first_lanes = lax.broadcasted_iota(jnp.int32, (LANES, LANES), 1) < HALO
    keep = jnp.where(first_lanes, keep_right, keep_left)
    rim = keep * rim_t_ref[0].astype(F32) + (1.0 - keep) * rim_t_ref[1].astype(F32)
    margin[...] = dot(line, rim.astype(BF16))
    margin_copies = to_neighbours(margin, margin_low, margin_high, 2)
    out_ref[...] = dot(line, mid_t[...])
    for copy in margin_copies:
        copy.wait_recv()
    out_ref[:, 0:LANES] += jnp.where(jnp.logical_and(side, tile > 0), margin_low[...], 0.0)
    out_ref[:, N - LANES : N] += jnp.where(
        jnp.logical_and(jnp.logical_not(side), tile < tiles - 1), margin_high[...], 0.0
    )
    for copy in spec_copies + halo_copies + part_copies + margin_copies:
        copy.wait_send()


def solution(mesh):
    ranks = mesh.shape["kern"]
    count = N // ranks
    mid, mid_t, rows_t, rim, rim_t = tables(ranks)

    def per_device(mask, orientation, target, kernel_real, kernel_imag, eigen_weights):
        hbm = pl.BlockSpec(memory_space=pl.ANY)
        vmem = pl.BlockSpec(memory_space=pltpu.VMEM)
        smem = pl.BlockSpec(memory_space=pltpu.SMEM)
        return pl.pallas_call(
            lambda *refs: body(ranks, *refs),
            out_shape=jax.ShapeDtypeStruct((count, N), F32),
            in_specs=[smem, smem] + [hbm] * 7 + [vmem] * 2,
            out_specs=vmem,
            scratch_shapes=[
                pltpu.VMEM((N, N), BF16),
                pltpu.VMEM((count, N), jnp.int32),
                pltpu.VMEM((KF, KF), F32),
                pltpu.VMEM((KF, KF), F32),
                pltpu.VMEM((N, LANES), BF16),
                pltpu.VMEM((LANES, N), BF16),
                pltpu.VMEM((count, LANES), BF16),
                pltpu.VMEM((LANES, count), BF16),
                pltpu.VMEM((ranks, KF, LANES), BF16),
                pltpu.VMEM((ranks, KF, LANES), BF16),
                pltpu.VMEM((LANES, LANES), BF16),
                pltpu.VMEM((LANES, LANES), BF16),
                pltpu.VMEM((LANES, LANES), BF16),
                pltpu.VMEM((LANES, N), BF16),
                pltpu.VMEM((LANES, ranks * LANES), BF16),
                pltpu.VMEM((N, LANES), BF16),
                pltpu.VMEM((CHUNKS, LANES, 2 * LANES), BF16),
                pltpu.VMEM((CHUNKS, 2 * LANES, LANES), BF16),
                pltpu.VMEM((N, 2 * LANES), BF16),
                pltpu.VMEM((N, LANES), F32),
                pltpu.VMEM((count, LANES), F32),
                pltpu.VMEM((count, LANES), F32),
                pltpu.VMEM((count, LANES), F32),
                pltpu.SemaphoreType.DMA((10,)),
                pltpu.SemaphoreType.DMA((ranks,)),
                pltpu.SemaphoreType.DMA((ranks,)),
                pltpu.SemaphoreType.DMA((ranks,)),
                pltpu.SemaphoreType.DMA((ranks,)),
                pltpu.SemaphoreType.DMA((4,)),
                pltpu.SemaphoreType.DMA((4,)),
            ],
            compiler_params=pltpu.CompilerParams(collective_id=0, has_side_effects=True),
        )(
            orientation,
            eigen_weights,
            mask,
            target,
            kernel_real,
            kernel_imag,
            jnp.asarray(mid),
            jnp.asarray(mid_t),
            jnp.asarray(rows_t),
            jnp.asarray(rim),
            jnp.asarray(rim_t),
        )

    in_specs = (
        P(None, "tile"),
        P("tile", None),
        P("kern", "tile"),
        P("kern", None, None),
        P("kern", None, None),
        P("kern"),
    )
    return jax.shard_map(
        per_device, mesh=mesh, in_specs=in_specs, out_specs=P("kern", "tile"), check_vma=False
    )
```

```python
import math

import jax
import jax.numpy as jnp
import ml_dtypes
import numpy as np
from jax import lax
from jax.experimental import pallas as pl
from jax.experimental.pallas import tpu as pltpu
from jax.sharding import PartitionSpec as P

N = 1152
HALO = 64
KF = 64
NE = 1280
LANES = 128
CHUNKS = N // LANES
GROUP = 2
BATCH = 4
HUBS = 2

STEEPNESS = 4.0
THRESHOLD = 1.0
F32 = jnp.float32
BF16 = jnp.bfloat16
MESH = pl.DeviceIdType.MESH


def wave_pair():
    phase = np.mod(np.arange(NE)[:, None] * (np.arange(KF) - KF // 2)[None, :], NE).astype(np.float32)
    phase = phase * np.float32(2.0 * math.pi / NE)
    return np.concatenate([np.cos(phase), np.sin(phase)], 1).astype(ml_dtypes.bfloat16)


def tables(ranks):
    full = wave_pair()
    mid = full[HALO : HALO + N]
    right, left = full[HALO + N :], full[:HALO]
    rim = np.stack([np.concatenate([right, left]), np.concatenate([right[::-1], left[::-1]])])
    rows_t = np.transpose(mid.reshape(ranks, N // ranks, 2 * KF), (0, 2, 1))
    return mid, mid.T.copy(), rows_t.copy(), rim, np.transpose(rim, (0, 2, 1)).copy()


def dot(a, b):
    return jnp.dot(a, b, preferred_element_type=F32)


def body(
    ranks,
    orient,
    weight,
    mask_hbm,
    target_hbm,
    hr_hbm,
    hi_hbm,
    mid_hbm,
    mid_t_hbm,
    rows_t_hbm,
    rim_ref,
    rim_t_ref,
    out_ref,
    mask,
    target,
    hr,
    hi,
    mid,
    mid_t,
    rows,
    rows_t,
    spec_all,
    part_all,
    strip,
    halo_low,
    halo_high,
    columns,
    stacked,
    intensity,
    whole,
    to_cols,
    from_cols,
    fields,
    partial,
    margin,
    margin_low,
    margin_high,
    local_sem,
    spec_send,
    spec_recv,
    part_send,
    part_recv,
    sum_send,
    sum_recv,
    tile_send,
    tile_recv,
):
    tiles = lax.axis_size("tile")
    tile = lax.axis_index("tile")
    rank = lax.axis_index("kern")
    up = lax.rem(tile + 1, tiles)
    down = lax.rem(tile + tiles - 1, tiles)
    count = N // ranks

    def load(src, dst, slot):
        copy = pltpu.make_async_copy(src, dst, local_sem.at[slot])
        copy.start()
        return copy

    barrier = pltpu.get_barrier_semaphore()
    for other in range(1, ranks):

        @pl.when(other > rank)
        def _():
            pl.semaphore_signal(barrier, inc=1, device_id={"kern": other}, device_id_type=MESH)

    for other in (up, down):
        pl.semaphore_signal(barrier, inc=1, device_id={"tile": other}, device_id_type=MESH)

    get_hr = load(hr_hbm.at[0], hr, 0)
    get_hi = load(hi_hbm.at[0], hi, 1)
    get_mid_t = load(mid_t_hbm, mid_t, 2)
    get_first = load(mask_hbm.at[:, 0:LANES], mask.at[:, 0:LANES], 3)
    get_last = load(mask_hbm.at[:, N - LANES : N], mask.at[:, N - LANES : N], 4)
    get_inner = load(mask_hbm.at[:, LANES : N - LANES], mask.at[:, LANES : N - LANES], 5)
    get_mid = load(mid_hbm, mid, 6)
    get_rows = load(mid_hbm.at[pl.ds(pl.multiple_of(rank * count, 16), count)], rows, 7)
    get_rows_t = load(rows_t_hbm.at[rank], rows_t, 8)
    get_target = load(target_hbm, target, 9)

    low = lax.broadcasted_iota(jnp.int32, (KF, 2 * KF), 1) < KF
    plus = jnp.where(low, 1.0, -1.0)
    minus = -plus

    def swap(x):
        return pltpu.roll(x, KF, 1)

    get_hr.wait()
    get_hi.wait()
    root = jnp.sqrt(jnp.full((KF, 2 * KF), weight[0, 0], F32))
    spec_all[rank] = (jnp.concatenate([hr[...], hi[...]], 1) * root).astype(BF16)

    pl.semaphore_wait(barrier, rank + 2)

    def spec_copy(source, other):
        return pltpu.make_async_remote_copy(
            src_ref=spec_all.at[source],
            dst_ref=spec_all.at[source],
            send_sem=spec_send.at[other],
            recv_sem=spec_recv.at[source],
            device_id={"kern": other},
            device_id_type=MESH,
        )

    for other in range(ranks - 1):

        @pl.when(other < rank)
        def _():
            spec_copy(rank, other).start()

    def to_neighbours(src, dst_up, dst_down, first):
        copies = []
        for place, (dst, other) in enumerate(((dst_up, up), (dst_down, down))):
            copy = pltpu.make_async_remote_copy(
                src_ref=src,
                dst_ref=dst,
                send_sem=tile_send.at[first + place],
                recv_sem=tile_recv.at[first + place],
                device_id={"tile": other},
                device_id_type=MESH,
            )
            copy.start()
            copies.append(copy)
        return copies

    get_mid_t.wait()
    get_first.wait()
    get_last.wait()
    first = dot(mid_t[...], mask[:, 0:LANES]).astype(BF16)
    last = dot(mid_t[...], mask[:, N - LANES : N]).astype(BF16)
    columns[:, 0:LANES] = first
    columns[:, N - LANES : N] = last
    edge = lax.broadcasted_iota(jnp.int32, (2 * KF, LANES), 1) < HALO
    strip[...] = jnp.where(edge, first.astype(F32), last.astype(F32)).astype(BF16)
    halo_copies = to_neighbours(strip, halo_low, halo_high, 0)

    get_inner.wait()
    for j in range(1, CHUNKS - 1):
        columns[:, j * LANES : (j + 1) * LANES] = dot(
            mid_t[...], mask[:, j * LANES : (j + 1) * LANES]
        ).astype(BF16)

    get_mid.wait()
    wide = lax.broadcasted_iota(jnp.int32, (LANES, 2 * KF), 1) < KF
    for j in range(CHUNKS):
        part = mid_t[:, j * LANES : (j + 1) * LANES]
        to_cols[j, 0:KF, 0:LANES] = part[:KF]
        to_cols[j, 0:KF, LANES:] = part[KF:]
        to_cols[j, KF:, 0:LANES] = -part[KF:]
        to_cols[j, KF:, LANES:] = part[:KF]
        block = mid[j * LANES : (j + 1) * LANES].astype(F32)
        from_cols[j, 0:LANES] = jnp.where(wide, block, -block).astype(BF16)
        from_cols[j, LANES:] = swap(block).astype(BF16)

    keep_right = orient[0, 1].astype(F32)
    keep_left = orient[0, 0].astype(F32)

    blocks = dot(columns[...], mid[...])
    upper = lax.broadcasted_iota(jnp.int32, (LANES, LANES), 0) < HALO
    keep = jnp.where(upper, keep_right, keep_left)
    rim = keep * rim_ref[0].astype(F32) + (1.0 - keep) * rim_ref[1].astype(F32)
    there = jnp.where(upper, jnp.where(tile < tiles - 1, 1.0, 0.0), jnp.where(tile > 0, 1.0, 0.0))
    rim = (rim * there).astype(BF16)
    for copy in halo_copies:
        copy.wait_recv()
    halo = jnp.where(edge, halo_high[...].astype(F32), halo_low[...].astype(F32)).astype(BF16)
    blocks = blocks + dot(halo, rim)
    lower = swap(blocks[KF:])
    spec = jnp.where(low, blocks[:KF] - lower, -(blocks[:KF] + lower)) * (1.0 / (NE * KF))
    spec_turned = swap(spec) * minus

    def kernel_parts(k):
        both = spec_all[k].astype(F32)
        other = swap(both)
        return jnp.where(low, both, other), jnp.where(low, other, both)

    get_rows.wait()
    intensity[...] = jnp.zeros_like(intensity)
    pair_rows = GROUP * count

    def arrive(i, carry):
        for k in range(GROUP):
            other = i * GROUP + k

            @pl.when(other != rank)
            def _():
                spec_copy(other, rank).wait_recv()

            @pl.when(other > rank)
            def _():
                spec_copy(rank, other).start()

            real, imag = kernel_parts(other)
            product = real * spec + imag * spec_turned
            stacked[0:KF, k * LANES : (k + 1) * LANES] = product.astype(BF16)
            stacked[KF:, k * LANES : (k + 1) * LANES] = (swap(product) * minus).astype(BF16)
        both = dot(rows[...], stacked[...]).astype(BF16)
        line = jnp.concatenate([both[:, k * LANES : (k + 1) * LANES] for k in range(GROUP)], 0)
        place = pl.ds(pl.multiple_of(i * pair_rows, 32), pair_rows)
        for j in range(CHUNKS):
            field = dot(line, to_cols[j])
            total = intensity[:, j * LANES : (j + 1) * LANES]
            for k in range(GROUP):
                one = field[k * count : (k + 1) * count]
                total = total + (one[:, :LANES] * one[:, :LANES] + one[:, LANES:] * one[:, LANES:])
            intensity[:, j * LANES : (j + 1) * LANES] = total
            fields[j, place] = field.astype(BF16)
        return carry

    lax.fori_loop(0, ranks // GROUP, arrive, 0)
    partial[...] = jnp.zeros_like(partial)
    get_target.wait()
    size = BATCH * count

    def chunk(j, carry):
        place = pl.ds(pl.multiple_of(j * LANES, LANES), LANES)
        total = intensity[:, place]
        resist = 1.0 / (1.0 + jnp.exp(-STEEPNESS * (total - THRESHOLD)))
        wanted = target[:, place].astype(F32)
        slope = (2.0 * (resist - wanted) * STEEPNESS * resist * (1.0 - resist)).astype(BF16)
        slope = jnp.concatenate([slope, slope], 1)
        slope = jnp.concatenate([slope] * BATCH, 0)
        for b in range(ranks // BATCH):
            weighted = fields[j, b * size : (b + 1) * size] * slope
            partial[b * size : (b + 1) * size] += dot(weighted, from_cols[j])
        return carry

    lax.fori_loop(0, CHUNKS, chunk, 0)

    get_rows_t.wait()
    grad = jnp.zeros((KF, 2 * KF), F32)
    for k in range(0, ranks, 2):
        pair = jnp.concatenate(
            [
                partial[k * count : (k + 1) * count].astype(BF16),
                partial[(k + 1) * count : (k + 2) * count].astype(BF16),
            ],
            1,
        )
        wave = dot(rows_t[...], pair)
        for i in range(2):
            one = wave[:, i * LANES : (i + 1) * LANES]
            one = one[:KF] + swap(one[KF:]) * plus
            real, imag = kernel_parts(k + i)
            grad = grad + real * one + imag * (swap(one) * plus)
    part_all[rank] = (grad * (2.0 / (NE * KF))).astype(BF16)

    def part_copy(source, hub):
        return pltpu.make_async_remote_copy(
            src_ref=part_all.at[source],
            dst_ref=part_all.at[source],
            send_sem=part_send.at[hub],
            recv_sem=part_recv.at[source],
            device_id={"kern": hub},
            device_id_type=MESH,
        )

    def sum_copy(other):
        return pltpu.make_async_remote_copy(
            src_ref=whole,
            dst_ref=whole,
            send_sem=sum_send.at[other],
            recv_sem=sum_recv.at[0],
            device_id={"kern": other},
            device_id_type=MESH,
        )

    for hub in range(HUBS):

        @pl.when(rank != hub)
        def _():
            part_copy(rank, hub).start()

    @pl.when(rank < HUBS)
    def _():
        total = jnp.zeros((KF, 2 * KF), F32)
        for source in range(ranks):

            @pl.when(source != rank)
            def _():
                part_copy(source, 0).wait_recv()

            total = total + part_all[source].astype(F32)
        whole[...] = total.astype(BF16)
        for step in range(1, ranks // HUBS):
            sum_copy(rank + step * HUBS).start()

    @pl.when(rank >= HUBS)
    def _():
        sum_copy(rank).wait_recv()

    grad = whole[...].astype(F32)
    both = jnp.concatenate([grad, swap(grad) * minus], 0).astype(BF16)
    line = dot(rows[...], both)
    side = lax.broadcasted_iota(jnp.int32, (count, 2 * KF), 1) < KF
    line = jnp.where(side, line, -line).astype(BF16)
    first_lanes = lax.broadcasted_iota(jnp.int32, (LANES, LANES), 1) < HALO
    keep = jnp.where(first_lanes, keep_right, keep_left)
    rim = keep * rim_t_ref[0].astype(F32) + (1.0 - keep) * rim_t_ref[1].astype(F32)
    margin[...] = dot(line, rim.astype(BF16))
    margin_copies = to_neighbours(margin, margin_low, margin_high, 2)
    out_ref[...] = dot(line, mid_t[...])
    for copy in margin_copies:
        copy.wait_recv()
    out_ref[:, 0:LANES] += jnp.where(jnp.logical_and(side, tile > 0), margin_low[...], 0.0)
    out_ref[:, N - LANES : N] += jnp.where(
        jnp.logical_and(jnp.logical_not(side), tile < tiles - 1), margin_high[...], 0.0
    )
    for copy in halo_copies + margin_copies:
        copy.wait_send()
    for other in range(ranks):

        @pl.when(other != rank)
        def _():
            spec_copy(rank, other).wait_send()

    for hub in range(HUBS):

        @pl.when(rank != hub)
        def _():
            part_copy(rank, hub).wait_send()

    @pl.when(rank < HUBS)
    def _():
        for step in range(1, ranks // HUBS):
            sum_copy(rank + step * HUBS).wait_send()


def solution(mesh):
    ranks = mesh.shape["kern"]
    count = N // ranks
    mid, mid_t, rows_t, rim, rim_t = tables(ranks)

    def per_device(mask, orientation, target, kernel_real, kernel_imag, eigen_weights):
        hbm = pl.BlockSpec(memory_space=pl.ANY)
        vmem = pl.BlockSpec(memory_space=pltpu.VMEM)
        smem = pl.BlockSpec(memory_space=pltpu.SMEM)
        return pl.pallas_call(
            lambda *refs: body(ranks, *refs),
            out_shape=jax.ShapeDtypeStruct((count, N), F32),
            in_specs=[smem, smem] + [hbm] * 7 + [vmem] * 2,
            out_specs=vmem,
            scratch_shapes=[
                pltpu.VMEM((N, N), BF16),
                pltpu.VMEM((count, N), jnp.int32),
                pltpu.VMEM((KF, KF), F32),
                pltpu.VMEM((KF, KF), F32),
                pltpu.VMEM((N, LANES), BF16),
                pltpu.VMEM((LANES, N), BF16),
                pltpu.VMEM((count, LANES), BF16),
                pltpu.VMEM((LANES, count), BF16),
                pltpu.VMEM((ranks, KF, LANES), BF16),
                pltpu.VMEM((ranks, KF, LANES), BF16),
                pltpu.VMEM((LANES, LANES), BF16),
                pltpu.VMEM((LANES, LANES), BF16),
                pltpu.VMEM((LANES, LANES), BF16),
                pltpu.VMEM((LANES, N), BF16),
                pltpu.VMEM((LANES, GROUP * LANES), BF16),
                pltpu.VMEM((count, N), F32),
                pltpu.VMEM((KF, LANES), BF16),
                pltpu.VMEM((CHUNKS, LANES, 2 * LANES), BF16),
                pltpu.VMEM((CHUNKS, 2 * LANES, LANES), BF16),
                pltpu.VMEM((CHUNKS, N, 2 * LANES), BF16),
                pltpu.VMEM((N, LANES), F32),
                pltpu.VMEM((count, LANES), F32),
                pltpu.VMEM((count, LANES), F32),
                pltpu.VMEM((count, LANES), F32),
                pltpu.SemaphoreType.DMA((10,)),
                pltpu.SemaphoreType.DMA((ranks,)),
                pltpu.SemaphoreType.DMA((ranks,)),
                pltpu.SemaphoreType.DMA((ranks,)),
                pltpu.SemaphoreType.DMA((ranks,)),
                pltpu.SemaphoreType.DMA((ranks,)),
                pltpu.SemaphoreType.DMA((1,)),
                pltpu.SemaphoreType.DMA((4,)),
                pltpu.SemaphoreType.DMA((4,)),
            ],
            compiler_params=pltpu.CompilerParams(collective_id=0, has_side_effects=True),
        )(
            orientation,
            eigen_weights.reshape(1, 1),
            mask,
            target,
            kernel_real,
            kernel_imag,
            jnp.asarray(mid),
            jnp.asarray(mid_t),
            jnp.asarray(rows_t),
            jnp.asarray(rim),
            jnp.asarray(rim_t),
        )

    in_specs = (
        P(None, "tile"),
        P("tile", None),
        P("kern", "tile"),
        P("kern", None, None),
        P("kern", None, None),
        P("kern"),
    )
    return jax.shard_map(
        per_device, mesh=mesh, in_specs=in_specs, out_specs=P("kern", "tile"), check_vma=False
    )
```

```python
import math

import jax
import jax.numpy as jnp
import ml_dtypes
import numpy as np
from jax import lax
from jax.experimental import pallas as pl
from jax.experimental.pallas import tpu as pltpu
from jax.sharding import PartitionSpec as P

N = 1152
HALO = 64
KF = 64
NE = 1280
LANES = 128
CHUNKS = N // LANES
GROUP = 2
BATCH = 4
HUBS = 2
LAST = 3

STEEPNESS = 4.0
THRESHOLD = 1.0
F32 = jnp.float32
BF16 = jnp.bfloat16
MESH = pl.DeviceIdType.MESH


def wave_pair():
    phase = np.mod(np.arange(NE)[:, None] * (np.arange(KF) - KF // 2)[None, :], NE).astype(np.float32)
    phase = phase * np.float32(2.0 * math.pi / NE)
    return np.concatenate([np.cos(phase), np.sin(phase)], 1).astype(ml_dtypes.bfloat16)


def tables(ranks):
    full = wave_pair()
    mid = full[HALO : HALO + N]
    right, left = full[HALO + N :], full[:HALO]
    rim = np.stack([np.concatenate([right, left]), np.concatenate([right[::-1], left[::-1]])])
    rows_t = np.transpose(mid.reshape(ranks, N // ranks, 2 * KF), (0, 2, 1))
    return mid, mid.T.copy(), rows_t.copy(), rim, np.transpose(rim, (0, 2, 1)).copy()


def dot(a, b):
    return jnp.dot(a, b, preferred_element_type=F32)


def body(
    ranks,
    orient,
    weight,
    mask_hbm,
    target_hbm,
    hr_hbm,
    hi_hbm,
    mid_hbm,
    mid_t_hbm,
    rows_t_hbm,
    rim_ref,
    rim_t_ref,
    out_ref,
    mask,
    target,
    hr,
    hi,
    mid,
    mid_t,
    rows,
    rows_t,
    spec_all,
    part_all,
    strip,
    halo_low,
    halo_high,
    columns,
    stacked,
    intensity,
    whole,
    to_cols,
    from_cols,
    fields,
    partial,
    margin,
    margin_low,
    margin_high,
    local_sem,
    spec_send,
    spec_recv,
    part_send,
    part_recv,
    sum_send,
    sum_recv,
    tile_send,
    tile_recv,
):
    tiles = lax.axis_size("tile")
    tile = lax.axis_index("tile")
    rank = lax.axis_index("kern")
    up = lax.rem(tile + 1, tiles)
    down = lax.rem(tile + tiles - 1, tiles)
    count = N // ranks

    def load(src, dst, slot):
        copy = pltpu.make_async_copy(src, dst, local_sem.at[slot])
        copy.start()
        return copy

    barrier = pltpu.get_barrier_semaphore()
    for other in range(1, ranks):

        @pl.when(other > rank)
        def _():
            pl.semaphore_signal(barrier, inc=1, device_id={"kern": other}, device_id_type=MESH)

    for other in (up, down):
        pl.semaphore_signal(barrier, inc=1, device_id={"tile": other}, device_id_type=MESH)

    get_hr = load(hr_hbm.at[0], hr, 0)
    get_hi = load(hi_hbm.at[0], hi, 1)
    get_mid_t = load(mid_t_hbm, mid_t, 2)
    get_first = load(mask_hbm.at[:, 0:LANES], mask.at[:, 0:LANES], 3)
    get_last = load(mask_hbm.at[:, N - LANES : N], mask.at[:, N - LANES : N], 4)
    get_inner = load(mask_hbm.at[:, LANES : N - LANES], mask.at[:, LANES : N - LANES], 5)
    get_mid = load(mid_hbm, mid, 6)
    get_rows = load(mid_hbm.at[pl.ds(pl.multiple_of(rank * count, 16), count)], rows, 7)
    get_rows_t = load(rows_t_hbm.at[rank], rows_t, 8)
    get_target = load(target_hbm, target, 9)

    low = lax.broadcasted_iota(jnp.int32, (KF, 2 * KF), 1) < KF
    plus = jnp.where(low, 1.0, -1.0)
    minus = -plus

    def swap(x):
        return pltpu.roll(x, KF, 1)

    get_hr.wait()
    get_hi.wait()
    root = jnp.sqrt(jnp.full((KF, 2 * KF), weight[0, 0], F32))
    spec_all[rank] = (jnp.concatenate([hr[...], hi[...]], 1) * root).astype(BF16)

    pl.semaphore_wait(barrier, rank + 2)

    def spec_copy(source, other):
        return pltpu.make_async_remote_copy(
            src_ref=spec_all.at[source],
            dst_ref=spec_all.at[source],
            send_sem=spec_send.at[other],
            recv_sem=spec_recv.at[source],
            device_id={"kern": other},
            device_id_type=MESH,
        )

    for other in range(ranks - 1):

        @pl.when(other < rank)
        def _():
            spec_copy(rank, other).start()

    def to_neighbours(src, dst_up, dst_down, first):
        copies = []
        for place, (dst, other) in enumerate(((dst_up, up), (dst_down, down))):
            copy = pltpu.make_async_remote_copy(
                src_ref=src,
                dst_ref=dst,
                send_sem=tile_send.at[first + place],
                recv_sem=tile_recv.at[first + place],
                device_id={"tile": other},
                device_id_type=MESH,
            )
            copy.start()
            copies.append(copy)
        return copies

    pairs = ranks // GROUP
    own = rank // GROUP
    late = pairs - LAST
    is_late = own >= late
    ahead = jnp.where(is_late, pairs - own, late - own)

    def turn(i):
        past = i - ahead
        nearest = jnp.where(past % 2 == 0, own - 1 - past // 2, past // 2)
        early = jnp.where(past < own, own - 1 - past, late + past - own)
        return jnp.where(past < 0, own + i, jnp.where(is_late, nearest, early))

    get_mid_t.wait()
    get_first.wait()
    get_last.wait()
    first = dot(mid_t[...], mask[:, 0:LANES]).astype(BF16)
    last = dot(mid_t[...], mask[:, N - LANES : N]).astype(BF16)
    columns[:, 0:LANES] = first
    columns[:, N - LANES : N] = last
    edge = lax.broadcasted_iota(jnp.int32, (2 * KF, LANES), 1) < HALO
    strip[...] = jnp.where(edge, first.astype(F32), last.astype(F32)).astype(BF16)
    halo_copies = to_neighbours(strip, halo_low, halo_high, 0)

    get_inner.wait()
    for j in range(1, CHUNKS - 1):
        columns[:, j * LANES : (j + 1) * LANES] = dot(
            mid_t[...], mask[:, j * LANES : (j + 1) * LANES]
        ).astype(BF16)

    get_mid.wait()
    wide = lax.broadcasted_iota(jnp.int32, (LANES, 2 * KF), 1) < KF
    for j in range(CHUNKS):
        part = mid_t[:, j * LANES : (j + 1) * LANES]
        to_cols[j, 0:KF, 0:LANES] = part[:KF]
        to_cols[j, 0:KF, LANES:] = part[KF:]
        to_cols[j, KF:, 0:LANES] = -part[KF:]
        to_cols[j, KF:, LANES:] = part[:KF]
        block = mid[j * LANES : (j + 1) * LANES].astype(F32)
        from_cols[j, 0:LANES] = jnp.where(wide, block, -block).astype(BF16)
        from_cols[j, LANES:] = swap(block).astype(BF16)

    keep_right = orient[0, 1].astype(F32)
    keep_left = orient[0, 0].astype(F32)

    blocks = dot(columns[...], mid[...])
    upper = lax.broadcasted_iota(jnp.int32, (LANES, LANES), 0) < HALO
    keep = jnp.where(upper, keep_right, keep_left)
    rim = keep * rim_ref[0].astype(F32) + (1.0 - keep) * rim_ref[1].astype(F32)
    there = jnp.where(upper, jnp.where(tile < tiles - 1, 1.0, 0.0), jnp.where(tile > 0, 1.0, 0.0))
    rim = (rim * there).astype(BF16)
    for copy in halo_copies:
        copy.wait_recv()
    halo = jnp.where(edge, halo_high[...].astype(F32), halo_low[...].astype(F32)).astype(BF16)
    blocks = blocks + dot(halo, rim)
    lower = swap(blocks[KF:])
    spec = jnp.where(low, blocks[:KF] - lower, -(blocks[:KF] + lower)) * (1.0 / (NE * KF))
    spec_turned = swap(spec) * minus

    def kernel_parts(k):
        both = spec_all[k].astype(F32)
        other = swap(both)
        return jnp.where(low, both, other), jnp.where(low, other, both)

    get_rows.wait()
    intensity[...] = jnp.zeros_like(intensity)
    pair_rows = GROUP * count

    def arrive(i, carry):
        at = turn(i)
        for k in range(GROUP):
            other = at * GROUP + k

            @pl.when(other != rank)
            def _():
                spec_copy(other, rank).wait_recv()

            @pl.when(other > rank)
            def _():
                spec_copy(rank, other).start()

            real, imag = kernel_parts(other)
            product = real * spec + imag * spec_turned
            stacked[0:KF, k * LANES : (k + 1) * LANES] = product.astype(BF16)
            stacked[KF:, k * LANES : (k + 1) * LANES] = (swap(product) * minus).astype(BF16)
        both = dot(rows[...], stacked[...]).astype(BF16)
        line = jnp.concatenate([both[:, k * LANES : (k + 1) * LANES] for k in range(GROUP)], 0)
        place = pl.ds(pl.multiple_of(i * pair_rows, 32), pair_rows)
        for j in range(CHUNKS):
            field = dot(line, to_cols[j])
            total = intensity[:, j * LANES : (j + 1) * LANES]
            for k in range(GROUP):
                one = field[k * count : (k + 1) * count]
                total = total + (one[:, :LANES] * one[:, :LANES] + one[:, LANES:] * one[:, LANES:])
            intensity[:, j * LANES : (j + 1) * LANES] = total
            fields[j, place] = field.astype(BF16)
        return carry

    lax.fori_loop(0, ranks // GROUP, arrive, 0)
    partial[...] = jnp.zeros_like(partial)
    get_target.wait()
    size = BATCH * count

    def chunk(j, carry):
        place = pl.ds(pl.multiple_of(j * LANES, LANES), LANES)
        total = intensity[:, place]
        resist = 1.0 / (1.0 + jnp.exp(-STEEPNESS * (total - THRESHOLD)))
        wanted = target[:, place].astype(F32)
        slope = (2.0 * (resist - wanted) * STEEPNESS * resist * (1.0 - resist)).astype(BF16)
        slope = jnp.concatenate([slope, slope], 1)
        slope = jnp.concatenate([slope] * BATCH, 0)
        for b in range(ranks // BATCH):
            weighted = fields[j, b * size : (b + 1) * size] * slope
            partial[b * size : (b + 1) * size] += dot(weighted, from_cols[j])
        return carry

    lax.fori_loop(0, CHUNKS, chunk, 0)

    get_rows_t.wait()
    grad = jnp.zeros((KF, 2 * KF), F32)
    for k in range(0, ranks, 2):
        pair = jnp.concatenate(
            [
                partial[k * count : (k + 1) * count].astype(BF16),
                partial[(k + 1) * count : (k + 2) * count].astype(BF16),
            ],
            1,
        )
        wave = dot(rows_t[...], pair)
        for i in range(2):
            one = wave[:, i * LANES : (i + 1) * LANES]
            one = one[:KF] + swap(one[KF:]) * plus
            real, imag = kernel_parts(turn(k // GROUP) * GROUP + i)
            grad = grad + real * one + imag * (swap(one) * plus)
    part_all[rank] = (grad * (2.0 / (NE * KF))).astype(BF16)

    def part_copy(source, hub):
        return pltpu.make_async_remote_copy(
            src_ref=part_all.at[source],
            dst_ref=part_all.at[source],
            send_sem=part_send.at[hub],
            recv_sem=part_recv.at[source],
            device_id={"kern": hub},
            device_id_type=MESH,
        )

    def sum_copy(other):
        return pltpu.make_async_remote_copy(
            src_ref=whole,
            dst_ref=whole,
            send_sem=sum_send.at[other],
            recv_sem=sum_recv.at[0],
            device_id={"kern": other},
            device_id_type=MESH,
        )

    for hub in range(HUBS):

        @pl.when(rank != hub)
        def _():
            part_copy(rank, hub).start()

    @pl.when(rank < HUBS)
    def _():
        total = jnp.zeros((KF, 2 * KF), F32)
        for source in range(ranks):

            @pl.when(source != rank)
            def _():
                part_copy(source, 0).wait_recv()

            total = total + part_all[source].astype(F32)
        whole[...] = total.astype(BF16)
        for step in range(1, ranks // HUBS):
            sum_copy(rank + step * HUBS).start()

    @pl.when(rank >= HUBS)
    def _():
        sum_copy(rank).wait_recv()

    grad = whole[...].astype(F32)
    both = jnp.concatenate([grad, swap(grad) * minus], 0).astype(BF16)
    line = dot(rows[...], both)
    side = lax.broadcasted_iota(jnp.int32, (count, 2 * KF), 1) < KF
    line = jnp.where(side, line, -line).astype(BF16)
    first_lanes = lax.broadcasted_iota(jnp.int32, (LANES, LANES), 1) < HALO
    keep = jnp.where(first_lanes, keep_right, keep_left)
    rim = keep * rim_t_ref[0].astype(F32) + (1.0 - keep) * rim_t_ref[1].astype(F32)
    margin[...] = dot(line, rim.astype(BF16))
    margin_copies = to_neighbours(margin, margin_low, margin_high, 2)
    out_ref[...] = dot(line, mid_t[...])
    for copy in margin_copies:
        copy.wait_recv()
    out_ref[:, 0:LANES] += jnp.where(jnp.logical_and(side, tile > 0), margin_low[...], 0.0)
    out_ref[:, N - LANES : N] += jnp.where(
        jnp.logical_and(jnp.logical_not(side), tile < tiles - 1), margin_high[...], 0.0
    )
    for copy in halo_copies + margin_copies:
        copy.wait_send()
    for other in range(ranks):

        @pl.when(other != rank)
        def _():
            spec_copy(rank, other).wait_send()

    for hub in range(HUBS):

        @pl.when(rank != hub)
        def _():
            part_copy(rank, hub).wait_send()

    @pl.when(rank < HUBS)
    def _():
        for step in range(1, ranks // HUBS):
            sum_copy(rank + step * HUBS).wait_send()


def solution(mesh):
    ranks = mesh.shape["kern"]
    count = N // ranks
    mid, mid_t, rows_t, rim, rim_t = tables(ranks)

    def per_device(mask, orientation, target, kernel_real, kernel_imag, eigen_weights):
        hbm = pl.BlockSpec(memory_space=pl.ANY)
        vmem = pl.BlockSpec(memory_space=pltpu.VMEM)
        smem = pl.BlockSpec(memory_space=pltpu.SMEM)
        return pl.pallas_call(
            lambda *refs: body(ranks, *refs),
            out_shape=jax.ShapeDtypeStruct((count, N), F32),
            in_specs=[smem, smem] + [hbm] * 7 + [vmem] * 2,
            out_specs=vmem,
            scratch_shapes=[
                pltpu.VMEM((N, N), BF16),
                pltpu.VMEM((count, N), jnp.int32),
                pltpu.VMEM((KF, KF), F32),
                pltpu.VMEM((KF, KF), F32),
                pltpu.VMEM((N, LANES), BF16),
                pltpu.VMEM((LANES, N), BF16),
                pltpu.VMEM((count, LANES), BF16),
                pltpu.VMEM((LANES, count), BF16),
                pltpu.VMEM((ranks, KF, LANES), BF16),
                pltpu.VMEM((ranks, KF, LANES), BF16),
                pltpu.VMEM((LANES, LANES), BF16),
                pltpu.VMEM((LANES, LANES), BF16),
                pltpu.VMEM((LANES, LANES), BF16),
                pltpu.VMEM((LANES, N), BF16),
                pltpu.VMEM((LANES, GROUP * LANES), BF16),
                pltpu.VMEM((count, N), F32),
                pltpu.VMEM((KF, LANES), BF16),
                pltpu.VMEM((CHUNKS, LANES, 2 * LANES), BF16),
                pltpu.VMEM((CHUNKS, 2 * LANES, LANES), BF16),
                pltpu.VMEM((CHUNKS, N, 2 * LANES), BF16),
                pltpu.VMEM((N, LANES), F32),
                pltpu.VMEM((count, LANES), F32),
                pltpu.VMEM((count, LANES), F32),
                pltpu.VMEM((count, LANES), F32),
                pltpu.SemaphoreType.DMA((10,)),
                pltpu.SemaphoreType.DMA((ranks,)),
                pltpu.SemaphoreType.DMA((ranks,)),
                pltpu.SemaphoreType.DMA((ranks,)),
                pltpu.SemaphoreType.DMA((ranks,)),
                pltpu.SemaphoreType.DMA((ranks,)),
                pltpu.SemaphoreType.DMA((1,)),
                pltpu.SemaphoreType.DMA((4,)),
                pltpu.SemaphoreType.DMA((4,)),
            ],
            compiler_params=pltpu.CompilerParams(collective_id=0, has_side_effects=True),
        )(
            orientation,
            eigen_weights.reshape(1, 1),
            mask,
            target,
            kernel_real,
            kernel_imag,
            jnp.asarray(mid),
            jnp.asarray(mid_t),
            jnp.asarray(rows_t),
            jnp.asarray(rim),
            jnp.asarray(rim_t),
        )

    in_specs = (
        P(None, "tile"),
        P("tile", None),
        P("kern", "tile"),
        P("kern", None, None),
        P("kern", None, None),
        P("kern"),
    )
    return jax.shard_map(
        per_device, mesh=mesh, in_specs=in_specs, out_specs=P("kern", "tile"), check_vma=False
    )
```

```python
import math

import jax
import jax.numpy as jnp
import ml_dtypes
import numpy as np
from jax import lax
from jax.experimental import pallas as pl
from jax.experimental.pallas import tpu as pltpu
from jax.sharding import PartitionSpec as P

N = 1152
HALO = 64
KF = 64
HALF = KF // 2
NE = 1280
LANES = 128
CHUNKS = N // LANES
GROUP = 2
BATCH = 4
LAST = 3
AHEAD = 3

STEEPNESS = 4.0
THRESHOLD = 1.0
F32 = jnp.float32
BF16 = jnp.bfloat16
MESH = pl.DeviceIdType.MESH


def wave_pair():
    phase = np.mod(np.arange(NE)[:, None] * (np.arange(KF) - KF // 2)[None, :], NE).astype(np.float32)
    phase = phase * np.float32(2.0 * math.pi / NE)
    return np.concatenate([np.cos(phase), np.sin(phase)], 1).astype(ml_dtypes.bfloat16)


def tables(ranks):
    full = wave_pair()
    mid = full[HALO : HALO + N]
    right, left = full[HALO + N :], full[:HALO]
    rim = np.stack([np.concatenate([right, left]), np.concatenate([right[::-1], left[::-1]])])
    rows_t = np.transpose(mid.reshape(ranks, N // ranks, 2 * KF), (0, 2, 1))
    return mid, mid.T.copy(), rows_t.copy(), rim, np.transpose(rim, (0, 2, 1)).copy()


def dot(a, b):
    return jnp.dot(a, b, preferred_element_type=F32)


def body(
    ranks,
    orient,
    weight,
    mask_hbm,
    target_hbm,
    hr_hbm,
    hi_hbm,
    mid_hbm,
    mid_t_hbm,
    rows_t_hbm,
    rim_ref,
    rim_t_ref,
    out_ref,
    mask,
    target,
    hr,
    hi,
    mid,
    mid_t,
    rows,
    rows_t,
    spec_all,
    part_all,
    share,
    window,
    strip,
    halo_low,
    halo_high,
    columns,
    stacked,
    intensity,
    to_cols,
    from_cols,
    fields,
    partial,
    margin,
    margin_low,
    margin_high,
    local_sem,
    spec_send,
    spec_recv,
    cross_send,
    cross_recv,
    part_send,
    part_recv,
    here,
    tile_send,
    tile_recv,
):
    tiles = lax.axis_size("tile")
    tile = lax.axis_index("tile")
    rank = lax.axis_index("kern")
    up = lax.rem(tile + 1, tiles)
    down = lax.rem(tile + tiles - 1, tiles)
    count = N // ranks

    def load(src, dst, slot):
        copy = pltpu.make_async_copy(src, dst, local_sem.at[slot])
        copy.start()
        return copy

    barrier = pltpu.get_barrier_semaphore()
    for other in range(1, ranks):

        @pl.when(other > rank)
        def _():
            pl.semaphore_signal(barrier, inc=1, device_id={"kern": other}, device_id_type=MESH)

    for other in (up, down):
        pl.semaphore_signal(barrier, inc=1, device_id={"tile": other}, device_id_type=MESH)

    get_hr = load(hr_hbm.at[0], hr, 0)
    get_hi = load(hi_hbm.at[0], hi, 1)
    get_mid_t = load(mid_t_hbm, mid_t, 2)
    get_first = load(mask_hbm.at[:, 0:LANES], mask.at[:, 0:LANES], 3)
    get_last = load(mask_hbm.at[:, N - LANES : N], mask.at[:, N - LANES : N], 4)
    get_inner = load(mask_hbm.at[:, LANES : N - LANES], mask.at[:, LANES : N - LANES], 5)
    get_mid = load(mid_hbm, mid, 6)
    get_rows = load(mid_hbm.at[pl.ds(pl.multiple_of(rank * count, 16), count)], rows, 7)
    get_rows_t = load(rows_t_hbm.at[rank], rows_t, 8)
    get_target = load(target_hbm, target, 9)

    low = lax.broadcasted_iota(jnp.int32, (KF, 2 * KF), 1) < KF
    plus = jnp.where(low, 1.0, -1.0)
    minus = -plus

    def swap(x):
        return pltpu.roll(x, KF, 1)

    pl.semaphore_wait(barrier, rank + 2)

    for other in range(ranks - 1):

        @pl.when(other < rank)
        def _():
            pl.semaphore_signal(here.at[rank], inc=1, device_id={"kern": other}, device_id_type=MESH)

    get_hr.wait()
    get_hi.wait()
    root = jnp.sqrt(jnp.full((KF, 2 * KF), weight[0, 0], F32))
    spectrum = (jnp.concatenate([hr[...], hi[...]], 1) * root).astype(BF16)
    spec_all[rank, 0] = spectrum[:HALF]
    spec_all[rank, 1] = spectrum[HALF:]
    core = lax.rem(tile, 2)

    def cross_copy(source):
        return pltpu.make_async_remote_copy(
            src_ref=spec_all.at[source, core],
            dst_ref=spec_all.at[source, core],
            send_sem=cross_send.at[source],
            recv_sem=cross_recv.at[source],
            device_id={"tile": tile + 1 - 2 * core},
            device_id_type=MESH,
        )

    def spec_copy(source, other):
        return pltpu.make_async_remote_copy(
            src_ref=spec_all.at[source, core],
            dst_ref=spec_all.at[source, core],
            send_sem=spec_send.at[other],
            recv_sem=spec_recv.at[source],
            device_id={"kern": other},
            device_id_type=MESH,
        )

    for other in range(ranks - 1):

        @pl.when(other < rank)
        def _():
            spec_copy(rank, other).start()

    def to_neighbours(src, dst_up, dst_down, first):
        copies = []
        for place, (dst, other) in enumerate(((dst_up, up), (dst_down, down))):
            copy = pltpu.make_async_remote_copy(
                src_ref=src,
                dst_ref=dst,
                send_sem=tile_send.at[first + place],
                recv_sem=tile_recv.at[first + place],
                device_id={"tile": other},
                device_id_type=MESH,
            )
            copy.start()
            copies.append(copy)
        return copies

    pairs = ranks // GROUP
    own = rank // GROUP
    ahead = pairs - own
    is_late = own >= pairs - LAST

    def turn(i):
        past = i - ahead
        nearest = jnp.where(past % 2 == 0, own - 1 - past // 2, past // 2)
        early = jnp.where(is_late, nearest, own - 1 - past)
        return jnp.where(past < 0, own + i, early)

    def relay(at):
        for k in range(GROUP):
            other = at * GROUP + k

            @pl.when(other != rank)
            def _():
                spec_copy(other, rank).wait_recv()
                cross_copy(other).start()

    def answer(at):
        for k in range(GROUP):
            other = at * GROUP + k

            @pl.when(jnp.logical_and(other > rank, other < ranks))
            def _():
                pl.semaphore_wait(here.at[other], 1)
                spec_copy(rank, other).start()

    get_mid_t.wait()
    get_first.wait()
    get_last.wait()
    first = dot(mid_t[...], mask[:, 0:LANES]).astype(BF16)
    last = dot(mid_t[...], mask[:, N - LANES : N]).astype(BF16)
    columns[:, 0:LANES] = first
    columns[:, N - LANES : N] = last
    edge = lax.broadcasted_iota(jnp.int32, (2 * KF, LANES), 1) < HALO
    strip[...] = jnp.where(edge, first.astype(F32), last.astype(F32)).astype(BF16)
    halo_copies = to_neighbours(strip, halo_low, halo_high, 0)

    get_inner.wait()
    for j in range(1, CHUNKS - 1):
        columns[:, j * LANES : (j + 1) * LANES] = dot(
            mid_t[...], mask[:, j * LANES : (j + 1) * LANES]
        ).astype(BF16)

    get_mid.wait()
    wide = lax.broadcasted_iota(jnp.int32, (LANES, 2 * KF), 1) < KF
    for j in range(CHUNKS):
        part = mid_t[:, j * LANES : (j + 1) * LANES]
        to_cols[j, 0:KF, 0:LANES] = part[:KF]
        to_cols[j, 0:KF, LANES:] = part[KF:]
        to_cols[j, KF:, 0:LANES] = -part[KF:]
        to_cols[j, KF:, LANES:] = part[:KF]
        block = mid[j * LANES : (j + 1) * LANES].astype(F32)
        from_cols[j, 0:LANES] = jnp.where(wide, block, -block).astype(BF16)
        from_cols[j, LANES:] = swap(block).astype(BF16)

    keep_right = orient[0, 1].astype(F32)
    keep_left = orient[0, 0].astype(F32)

    blocks = dot(columns[...], mid[...])
    upper = lax.broadcasted_iota(jnp.int32, (LANES, LANES), 0) < HALO
    keep = jnp.where(upper, keep_right, keep_left)
    rim = keep * rim_ref[0].astype(F32) + (1.0 - keep) * rim_ref[1].astype(F32)
    there = jnp.where(upper, jnp.where(tile < tiles - 1, 1.0, 0.0), jnp.where(tile > 0, 1.0, 0.0))
    rim = (rim * there).astype(BF16)
    for copy in halo_copies:
        copy.wait_recv()
    halo = jnp.where(edge, halo_high[...].astype(F32), halo_low[...].astype(F32)).astype(BF16)
    blocks = blocks + dot(halo, rim)
    lower = swap(blocks[KF:])
    spec = jnp.where(low, blocks[:KF] - lower, -(blocks[:KF] + lower)) * (1.0 / (NE * KF))
    spec_turned = swap(spec) * minus

    def kernel_parts(k):
        both = spec_all[k].reshape(KF, 2 * KF).astype(F32)
        other = swap(both)
        return jnp.where(low, both, other), jnp.where(low, other, both)

    get_rows.wait()
    intensity[...] = jnp.zeros_like(intensity)
    pair_rows = GROUP * count

    def arrive(i, carry):
        at = turn(i)
        answer(own + i + AHEAD)

        @pl.when(i + 1 < pairs)
        def _():
            relay(turn(i + 1))

        for k in range(GROUP):
            other = at * GROUP + k

            @pl.when(other != rank)
            def _():
                cross_copy(other).wait_recv()

            real, imag = kernel_parts(other)
            product = real * spec + imag * spec_turned
            stacked[0:KF, k * LANES : (k + 1) * LANES] = product.astype(BF16)
            stacked[KF:, k * LANES : (k + 1) * LANES] = (swap(product) * minus).astype(BF16)
        both = dot(rows[...], stacked[...]).astype(BF16)
        line = jnp.concatenate([both[:, k * LANES : (k + 1) * LANES] for k in range(GROUP)], 0)
        place = pl.ds(pl.multiple_of(i * pair_rows, 32), pair_rows)
        for j in range(CHUNKS):
            field = dot(line, to_cols[j])
            total = intensity[:, j * LANES : (j + 1) * LANES]
            for k in range(GROUP):
                one = field[k * count : (k + 1) * count]
                total = total + (one[:, :LANES] * one[:, :LANES] + one[:, LANES:] * one[:, LANES:])
            intensity[:, j * LANES : (j + 1) * LANES] = total
            fields[j, place] = field.astype(BF16)
        return carry

    for i in range(AHEAD):
        answer(own + i)
    relay(own)
    lax.fori_loop(0, ranks // GROUP, arrive, 0)
    partial[...] = jnp.zeros_like(partial)
    get_target.wait()
    size = BATCH * count

    def chunk(j, carry):
        place = pl.ds(pl.multiple_of(j * LANES, LANES), LANES)
        total = intensity[:, place]
        resist = 1.0 / (1.0 + jnp.exp(-STEEPNESS * (total - THRESHOLD)))
        wanted = target[:, place].astype(F32)
        slope = (2.0 * (resist - wanted) * STEEPNESS * resist * (1.0 - resist)).astype(BF16)
        slope = jnp.concatenate([slope, slope], 1)
        slope = jnp.concatenate([slope] * BATCH, 0)
        for b in range(ranks // BATCH):
            weighted = fields[j, b * size : (b + 1) * size] * slope
            partial[b * size : (b + 1) * size] += dot(weighted, from_cols[j])
        return carry

    lax.fori_loop(0, CHUNKS, chunk, 0)

    get_rows_t.wait()
    grad = jnp.zeros((KF, 2 * KF), F32)
    for k in range(0, ranks, 2):
        pair = jnp.concatenate(
            [
                partial[k * count : (k + 1) * count].astype(BF16),
                partial[(k + 1) * count : (k + 2) * count].astype(BF16),
            ],
            1,
        )
        wave = dot(rows_t[...], pair)
        for i in range(2):
            one = wave[:, i * LANES : (i + 1) * LANES]
            one = one[:KF] + swap(one[KF:]) * plus
            real, imag = kernel_parts(turn(k // GROUP) * GROUP + i)
            grad = grad + real * one + imag * (swap(one) * plus)
    def ring_copy(src, slot, turn_by, flip):
        to = lax.rem(own + turn_by, pairs) * GROUP + (lax.rem(rank, GROUP) if not flip else 1 - lax.rem(rank, GROUP))
        copy = pltpu.make_async_remote_copy(
            src_ref=src,
            dst_ref=part_all.at[slot],
            send_sem=part_send.at[slot],
            recv_sem=part_recv.at[slot],
            device_id={"kern": to},
            device_id_type=MESH,
        )
        copy.start()
        return copy

    share[...] = (grad * (2.0 / (NE * KF))).astype(BF16)
    near = [
        ring_copy(share, slot, turn_by, flip)
        for slot, (turn_by, flip) in enumerate(
            ((pairs - 1, False), (pairs - 1, True), (1, False), (1, True), (0, True))
        )
    ]
    total = share[...].astype(F32)
    for slot, copy in enumerate(near):
        copy.wait_recv()
        total = total + part_all[slot].astype(F32)
    window[...] = total.astype(BF16)
    far = [
        ring_copy(window, len(near) + slot, turn_by, False)
        for slot, turn_by in enumerate((pairs // 2, pairs // 4, pairs - pairs // 4))
    ]
    for slot, copy in enumerate(far):
        copy.wait_recv()
        total = total + part_all[len(near) + slot].astype(F32)
    grad = total.astype(BF16).astype(F32)
    both = jnp.concatenate([grad, swap(grad) * minus], 0).astype(BF16)
    line = dot(rows[...], both)
    side = lax.broadcasted_iota(jnp.int32, (count, 2 * KF), 1) < KF
    line = jnp.where(side, line, -line).astype(BF16)
    first_lanes = lax.broadcasted_iota(jnp.int32, (LANES, LANES), 1) < HALO
    keep = jnp.where(first_lanes, keep_right, keep_left)
    rim = keep * rim_t_ref[0].astype(F32) + (1.0 - keep) * rim_t_ref[1].astype(F32)
    margin[...] = dot(line, rim.astype(BF16))
    margin_copies = to_neighbours(margin, margin_low, margin_high, 2)
    out_ref[...] = dot(line, mid_t[...])
    for copy in margin_copies:
        copy.wait_recv()
    out_ref[:, 0:LANES] += jnp.where(jnp.logical_and(side, tile > 0), margin_low[...], 0.0)
    out_ref[:, N - LANES : N] += jnp.where(
        jnp.logical_and(jnp.logical_not(side), tile < tiles - 1), margin_high[...], 0.0
    )
    for copy in halo_copies + near + far + margin_copies:
        copy.wait_send()
    for other in range(ranks):

        @pl.when(other != rank)
        def _():
            spec_copy(rank, other).wait_send()
            cross_copy(other).wait_send()


def solution(mesh):
    ranks = mesh.shape["kern"]
    count = N // ranks
    mid, mid_t, rows_t, rim, rim_t = tables(ranks)

    def per_device(mask, orientation, target, kernel_real, kernel_imag, eigen_weights):
        hbm = pl.BlockSpec(memory_space=pl.ANY)
        vmem = pl.BlockSpec(memory_space=pltpu.VMEM)
        smem = pl.BlockSpec(memory_space=pltpu.SMEM)
        return pl.pallas_call(
            lambda *refs: body(ranks, *refs),
            out_shape=jax.ShapeDtypeStruct((count, N), F32),
            in_specs=[smem, smem] + [hbm] * 7 + [vmem] * 2,
            out_specs=vmem,
            scratch_shapes=[
                pltpu.VMEM((N, N), BF16),
                pltpu.VMEM((count, N), jnp.int32),
                pltpu.VMEM((KF, KF), F32),
                pltpu.VMEM((KF, KF), F32),
                pltpu.VMEM((N, LANES), BF16),
                pltpu.VMEM((LANES, N), BF16),
                pltpu.VMEM((count, LANES), BF16),
                pltpu.VMEM((LANES, count), BF16),
                pltpu.VMEM((ranks, 2, HALF, LANES), BF16),
                pltpu.VMEM((8, KF, LANES), BF16),
                pltpu.VMEM((KF, LANES), BF16),
                pltpu.VMEM((KF, LANES), BF16),
                pltpu.VMEM((LANES, LANES), BF16),
                pltpu.VMEM((LANES, LANES), BF16),
                pltpu.VMEM((LANES, LANES), BF16),
                pltpu.VMEM((LANES, N), BF16),
                pltpu.VMEM((LANES, GROUP * LANES), BF16),
                pltpu.VMEM((count, N), F32),
                pltpu.VMEM((CHUNKS, LANES, 2 * LANES), BF16),
                pltpu.VMEM((CHUNKS, 2 * LANES, LANES), BF16),
                pltpu.VMEM((CHUNKS, N, 2 * LANES), BF16),
                pltpu.VMEM((N, LANES), F32),
                pltpu.VMEM((count, LANES), F32),
                pltpu.VMEM((count, LANES), F32),
                pltpu.VMEM((count, LANES), F32),
                pltpu.SemaphoreType.DMA((10,)),
                pltpu.SemaphoreType.DMA((ranks,)),
                pltpu.SemaphoreType.DMA((ranks,)),
                pltpu.SemaphoreType.DMA((ranks,)),
                pltpu.SemaphoreType.DMA((ranks,)),
                pltpu.SemaphoreType.DMA((ranks,)),
                pltpu.SemaphoreType.DMA((ranks,)),
                pltpu.SemaphoreType.REGULAR((ranks,)),
                pltpu.SemaphoreType.DMA((4,)),
                pltpu.SemaphoreType.DMA((4,)),
            ],
            compiler_params=pltpu.CompilerParams(collective_id=0, has_side_effects=True),
        )(
            orientation,
            eigen_weights.reshape(1, 1),
            mask,
            target,
            kernel_real,
            kernel_imag,
            jnp.asarray(mid),
            jnp.asarray(mid_t),
            jnp.asarray(rows_t),
            jnp.asarray(rim),
            jnp.asarray(rim_t),
        )

    in_specs = (
        P(None, "tile"),
        P("tile", None),
        P("kern", "tile"),
        P("kern", None, None),
        P("kern", None, None),
        P("kern"),
    )
    return jax.shard_map(
        per_device, mesh=mesh, in_specs=in_specs, out_specs=P("kern", "tile"), check_vma=False
    )
```

```python
import math

import jax
import jax.numpy as jnp
import ml_dtypes
import numpy as np
from jax import lax
from jax.experimental import pallas as pl
from jax.experimental.pallas import tpu as pltpu
from jax.sharding import PartitionSpec as P

N = 1152
HALO = 64
KF = 64
HALF = KF // 2
NE = 1280
LANES = 128
CHUNKS = N // LANES
GROUP = 2
BATCH = 4
AHEAD = 3
HELPED = 4

STEEPNESS = 4.0
THRESHOLD = 1.0
F32 = jnp.float32
BF16 = jnp.bfloat16
MESH = pl.DeviceIdType.MESH


def wave_pair():
    phase = np.mod(np.arange(NE)[:, None] * (np.arange(KF) - KF // 2)[None, :], NE).astype(np.float32)
    phase = phase * np.float32(2.0 * math.pi / NE)
    return np.concatenate([np.cos(phase), np.sin(phase)], 1).astype(ml_dtypes.bfloat16)


def tables(ranks):
    full = wave_pair()
    mid = full[HALO : HALO + N]
    right, left = full[HALO + N :], full[:HALO]
    rim = np.stack([np.concatenate([right, left]), np.concatenate([right[::-1], left[::-1]])])
    rows_t = np.transpose(mid.reshape(ranks, N // ranks, 2 * KF), (0, 2, 1))
    return mid, mid.T.copy(), rows_t.copy(), rim, np.transpose(rim, (0, 2, 1)).copy()


def dot(a, b):
    return jnp.dot(a, b, preferred_element_type=F32)


def body(
    ranks,
    orient,
    weight,
    mask_hbm,
    target_hbm,
    hr_hbm,
    hi_hbm,
    mid_hbm,
    mid_t_hbm,
    rows_t_hbm,
    rim_ref,
    rim_t_ref,
    out_ref,
    mask,
    target,
    wanted,
    hr,
    hi,
    mid,
    mid_t,
    rows,
    rows_t,
    spec_all,
    part_all,
    share,
    window,
    strip,
    halo_low,
    halo_high,
    columns,
    stacked,
    intensity,
    to_cols,
    from_cols,
    fields,
    partial,
    gradient,
    margin,
    margin_low,
    margin_high,
    local_sem,
    spec_send,
    spec_recv,
    cross_send,
    cross_recv,
    part_send,
    part_recv,
    here,
    target_sem,
    tile_send,
    tile_recv,
):
    tiles = lax.axis_size("tile")
    tile = lax.axis_index("tile")
    rank = lax.axis_index("kern")
    up = lax.rem(tile + 1, tiles)
    down = lax.rem(tile + tiles - 1, tiles)
    count = N // ranks

    def load(src, dst, slot):
        copy = pltpu.make_async_copy(src, dst, local_sem.at[slot])
        copy.start()
        return copy

    barrier = pltpu.get_barrier_semaphore()
    for other in range(1, ranks):

        @pl.when(other > rank)
        def _():
            pl.semaphore_signal(barrier, inc=1, device_id={"kern": other}, device_id_type=MESH)

    for other in (up, down):
        pl.semaphore_signal(barrier, inc=1, device_id={"tile": other}, device_id_type=MESH)

    get_hr = load(hr_hbm.at[0], hr, 0)
    get_hi = load(hi_hbm.at[0], hi, 1)
    get_mid_t = load(mid_t_hbm, mid_t, 2)
    get_first = load(mask_hbm.at[:, 0:LANES], mask.at[:, 0:LANES], 3)
    get_last = load(mask_hbm.at[:, N - LANES : N], mask.at[:, N - LANES : N], 4)
    get_inner = load(mask_hbm.at[:, LANES : N - LANES], mask.at[:, LANES : N - LANES], 5)
    get_mid = load(mid_hbm, mid, 6)
    get_target = load(target_hbm, target, 7)
    workers = ranks - HELPED
    whose = (rank, lax.rem(rank + workers, ranks))
    get_rows = [
        load(mid_hbm.at[pl.ds(pl.multiple_of(owner * count, 16), count)], rows.at[s], 8 + s)
        for s, owner in enumerate(whose)
    ]
    get_rows_t = [load(rows_t_hbm.at[owner], rows_t.at[s], 10 + s) for s, owner in enumerate(whose)]

    low = lax.broadcasted_iota(jnp.int32, (KF, 2 * KF), 1) < KF
    plus = jnp.where(low, 1.0, -1.0)
    minus = -plus

    def swap(x):
        return pltpu.roll(x, KF, 1)

    pl.semaphore_wait(barrier, rank + 2)

    for other in range(ranks - 1):

        @pl.when(jnp.logical_and(other < rank, jnp.logical_or(rank < workers, other >= workers)))
        def _():
            pl.semaphore_signal(here.at[rank], inc=1, device_id={"kern": other}, device_id_type=MESH)

    get_hr.wait()
    get_hi.wait()
    root = jnp.sqrt(jnp.full((KF, 2 * KF), weight[0, 0], F32))
    spectrum = (jnp.concatenate([hr[...], hi[...]], 1) * root).astype(BF16)
    spec_all[rank, 0] = spectrum[:HALF]
    spec_all[rank, 1] = spectrum[HALF:]
    core = lax.rem(tile, 2)

    def cross_copy(source):
        return pltpu.make_async_remote_copy(
            src_ref=spec_all.at[source, core],
            dst_ref=spec_all.at[source, core],
            send_sem=cross_send.at[source],
            recv_sem=cross_recv.at[source],
            device_id={"tile": tile + 1 - 2 * core},
            device_id_type=MESH,
        )

    def spec_copy(source, other):
        return pltpu.make_async_remote_copy(
            src_ref=spec_all.at[source, core],
            dst_ref=spec_all.at[source, core],
            send_sem=spec_send.at[other],
            recv_sem=spec_recv.at[source],
            device_id={"kern": other},
            device_id_type=MESH,
        )

    for other in range(workers):

        @pl.when(other < rank)
        def _():
            spec_copy(rank, other).start()

    def to_neighbours(src, dst_up, dst_down, first):
        copies = []
        for place, (dst, other) in enumerate(((dst_up, up), (dst_down, down))):
            copy = pltpu.make_async_remote_copy(
                src_ref=src,
                dst_ref=dst,
                send_sem=tile_send.at[first + place],
                recv_sem=tile_recv.at[first + place],
                device_id={"tile": other},
                device_id_type=MESH,
            )
            copy.start()
            copies.append(copy)
        return copies

    pairs = ranks // GROUP
    own = rank // GROUP
    ahead = pairs - own

    def turn(i):
        past = i - ahead
        return jnp.where(past < 0, own + i, own - 1 - past)

    def relay(at):
        for k in range(GROUP):
            other = at * GROUP + k

            @pl.when(other != rank)
            def _():
                spec_copy(other, rank).wait_recv()
                cross_copy(other).start()

    def answer(at):
        for k in range(GROUP):
            other = at * GROUP + k

            @pl.when(jnp.logical_and(other > rank, other < workers))
            def _():
                pl.semaphore_wait(here.at[other], 1)
                spec_copy(rank, other).start()

    get_mid_t.wait()
    get_first.wait()
    get_last.wait()
    first = dot(mid_t[...], mask[:, 0:LANES]).astype(BF16)
    last = dot(mid_t[...], mask[:, N - LANES : N]).astype(BF16)
    columns[:, 0:LANES] = first
    columns[:, N - LANES : N] = last
    edge = lax.broadcasted_iota(jnp.int32, (2 * KF, LANES), 1) < HALO
    strip[...] = jnp.where(edge, first.astype(F32), last.astype(F32)).astype(BF16)
    halo_copies = to_neighbours(strip, halo_low, halo_high, 0)

    get_inner.wait()
    for j in range(1, CHUNKS - 1):
        columns[:, j * LANES : (j + 1) * LANES] = dot(
            mid_t[...], mask[:, j * LANES : (j + 1) * LANES]
        ).astype(BF16)

    get_mid.wait()
    wide = lax.broadcasted_iota(jnp.int32, (LANES, 2 * KF), 1) < KF
    for j in range(CHUNKS):
        part = mid_t[:, j * LANES : (j + 1) * LANES]
        to_cols[j, 0:KF, 0:LANES] = part[:KF]
        to_cols[j, 0:KF, LANES:] = part[KF:]
        to_cols[j, KF:, 0:LANES] = -part[KF:]
        to_cols[j, KF:, LANES:] = part[:KF]
        block = mid[j * LANES : (j + 1) * LANES].astype(F32)
        from_cols[j, 0:LANES] = jnp.where(wide, block, -block).astype(BF16)
        from_cols[j, LANES:] = swap(block).astype(BF16)

    keep_right = orient[0, 1].astype(F32)
    keep_left = orient[0, 0].astype(F32)

    blocks = dot(columns[...], mid[...])
    upper = lax.broadcasted_iota(jnp.int32, (LANES, LANES), 0) < HALO
    keep = jnp.where(upper, keep_right, keep_left)
    rim = keep * rim_ref[0].astype(F32) + (1.0 - keep) * rim_ref[1].astype(F32)
    there = jnp.where(upper, jnp.where(tile < tiles - 1, 1.0, 0.0), jnp.where(tile > 0, 1.0, 0.0))
    rim = (rim * there).astype(BF16)
    for copy in halo_copies:
        copy.wait_recv()
    halo = jnp.where(edge, halo_high[...].astype(F32), halo_low[...].astype(F32)).astype(BF16)
    blocks = blocks + dot(halo, rim)
    lower = swap(blocks[KF:])
    spec = jnp.where(low, blocks[:KF] - lower, -(blocks[:KF] + lower)) * (1.0 / (NE * KF))
    spec_turned = swap(spec) * minus

    def kernel_parts(k):
        both = spec_all[k].reshape(KF, 2 * KF).astype(F32)
        other = swap(both)
        return jnp.where(low, both, other), jnp.where(low, other, both)

    for copy in [get_target] + get_rows + get_rows_t:
        copy.wait()
    wanted[0] = target[...].astype(F32).astype(BF16)
    target_copy = pltpu.make_async_remote_copy(
        src_ref=wanted.at[0],
        dst_ref=wanted.at[1],
        send_sem=target_sem.at[0],
        recv_sem=target_sem.at[1],
        device_id={"kern": lax.rem(rank + HELPED, ranks)},
        device_id_type=MESH,
    )

    @pl.when(rank >= workers)
    def _():
        for other in range(workers):
            spec_copy(rank, other).wait_send()
        target_copy.start()

    pair_rows = GROUP * count

    def forward(i, s):
        both = dot(rows[s], stacked[...]).astype(BF16)
        line = jnp.concatenate([both[:, k * LANES : (k + 1) * LANES] for k in range(GROUP)], 0)
        place = pl.ds(pl.multiple_of(i * pair_rows, 32), pair_rows)
        for j in range(CHUNKS):
            field = dot(line, to_cols[j])
            total = intensity[s, :, j * LANES : (j + 1) * LANES]
            for k in range(GROUP):
                one = field[k * count : (k + 1) * count]
                total = total + (one[:, :LANES] * one[:, :LANES] + one[:, LANES:] * one[:, LANES:])
            intensity[s, :, j * LANES : (j + 1) * LANES] = total
            fields[s, j, place] = field.astype(BF16)

    def arrive(i, carry):
        at = turn(i)
        answer(own + i + AHEAD)

        @pl.when(i + 1 < pairs)
        def _():
            relay(turn(i + 1))

        for k in range(GROUP):
            other = at * GROUP + k

            @pl.when(other != rank)
            def _():
                cross_copy(other).wait_recv()

            real, imag = kernel_parts(other)
            product = real * spec + imag * spec_turned
            stacked[0:KF, k * LANES : (k + 1) * LANES] = product.astype(BF16)
            stacked[KF:, k * LANES : (k + 1) * LANES] = (swap(product) * minus).astype(BF16)
        forward(i, 0)

        @pl.when(rank < HELPED)
        def _():
            forward(i, 1)

        return carry

    size = BATCH * count

    def adjoint(s):
        def chunk(j, carry):
            place = pl.ds(pl.multiple_of(j * LANES, LANES), LANES)
            total = intensity[s, :, place]
            resist = 1.0 / (1.0 + jnp.exp(-STEEPNESS * (total - THRESHOLD)))
            pattern = wanted[s, :, place].astype(F32)
            slope = (2.0 * (resist - pattern) * STEEPNESS * resist * (1.0 - resist)).astype(BF16)
            slope = jnp.concatenate([slope, slope], 1)
            slope = jnp.concatenate([slope] * BATCH, 0)
            for b in range(ranks // BATCH):
                weighted = fields[s, j, b * size : (b + 1) * size] * slope
                partial[b * size : (b + 1) * size] += dot(weighted, from_cols[j])
            return carry

        partial[...] = jnp.zeros_like(partial)
        lax.fori_loop(0, CHUNKS, chunk, 0)

        grad = jnp.zeros((KF, 2 * KF), F32)
        for k in range(0, ranks, 2):
            pair = [partial[(k + i) * count : (k + i + 1) * count].astype(BF16) for i in range(2)]
            wave = dot(rows_t[s], jnp.concatenate(pair, 1))
            for i in range(2):
                one = wave[:, i * LANES : (i + 1) * LANES]
                one = one[:KF] + swap(one[KF:]) * plus
                real, imag = kernel_parts(turn(k // GROUP) * GROUP + i)
                grad = grad + real * one + imag * (swap(one) * plus)
        gradient[...] += grad * (2.0 / (NE * KF))

    gradient[...] = jnp.zeros_like(gradient)

    @pl.when(rank < workers)
    def _():
        intensity[...] = jnp.zeros_like(intensity)
        for i in range(AHEAD):
            answer(own + i)
        relay(own)
        lax.fori_loop(0, pairs, arrive, 0)
        adjoint(0)

    @pl.when(rank < HELPED)
    def _():
        target_copy.wait_recv()
        adjoint(1)

    def ring_copy(src, slot, turn_by, flip):
        to = lax.rem(own + turn_by, pairs) * GROUP + (lax.rem(rank, GROUP) if not flip else 1 - lax.rem(rank, GROUP))
        copy = pltpu.make_async_remote_copy(
            src_ref=src,
            dst_ref=part_all.at[slot],
            send_sem=part_send.at[slot],
            recv_sem=part_recv.at[slot],
            device_id={"kern": to},
            device_id_type=MESH,
        )
        copy.start()
        return copy

    for other in range(workers + 1, ranks):

        @pl.when(jnp.logical_and(rank >= workers, other > rank))
        def _():
            pl.semaphore_wait(here.at[other], 1)

    share[...] = gradient[...].astype(BF16)
    near = [
        ring_copy(share, slot, turn_by, flip)
        for slot, (turn_by, flip) in enumerate(
            ((pairs - 1, False), (pairs - 1, True), (1, False), (1, True), (0, True))
        )
    ]
    total = share[...].astype(F32)
    for slot, copy in enumerate(near):
        copy.wait_recv()
        total = total + part_all[slot].astype(F32)
    window[...] = total.astype(BF16)
    far = [
        ring_copy(window, len(near) + slot, turn_by, False)
        for slot, turn_by in enumerate((pairs // 2, pairs // 4, pairs - pairs // 4))
    ]
    for slot, copy in enumerate(far):
        copy.wait_recv()
        total = total + part_all[len(near) + slot].astype(F32)
    grad = total.astype(BF16).astype(F32)
    both = jnp.concatenate([grad, swap(grad) * minus], 0).astype(BF16)
    line = dot(rows[0], both)
    side = lax.broadcasted_iota(jnp.int32, (count, 2 * KF), 1) < KF
    line = jnp.where(side, line, -line).astype(BF16)
    first_lanes = lax.broadcasted_iota(jnp.int32, (LANES, LANES), 1) < HALO
    keep = jnp.where(first_lanes, keep_right, keep_left)
    rim = keep * rim_t_ref[0].astype(F32) + (1.0 - keep) * rim_t_ref[1].astype(F32)
    margin[...] = dot(line, rim.astype(BF16))
    margin_copies = to_neighbours(margin, margin_low, margin_high, 2)
    out_ref[...] = dot(line, mid_t[...])
    for copy in margin_copies:
        copy.wait_recv()
    out_ref[:, 0:LANES] += jnp.where(jnp.logical_and(side, tile > 0), margin_low[...], 0.0)
    out_ref[:, N - LANES : N] += jnp.where(
        jnp.logical_and(jnp.logical_not(side), tile < tiles - 1), margin_high[...], 0.0
    )
    for copy in halo_copies + near + far + margin_copies:
        copy.wait_send()

    @pl.when(rank >= workers)
    def _():
        target_copy.wait_send()

    for other in range(workers):

        @pl.when(jnp.logical_and(other != rank, rank < workers))
        def _():
            spec_copy(rank, other).wait_send()

    for other in range(ranks):

        @pl.when(jnp.logical_and(other != rank, rank < workers))
        def _():
            cross_copy(other).wait_send()


def solution(mesh):
    ranks = mesh.shape["kern"]
    count = N // ranks
    mid, mid_t, rows_t, rim, rim_t = tables(ranks)

    def per_device(mask, orientation, target, kernel_real, kernel_imag, eigen_weights):
        hbm = pl.BlockSpec(memory_space=pl.ANY)
        vmem = pl.BlockSpec(memory_space=pltpu.VMEM)
        smem = pl.BlockSpec(memory_space=pltpu.SMEM)
        return pl.pallas_call(
            lambda *refs: body(ranks, *refs),
            out_shape=jax.ShapeDtypeStruct((count, N), F32),
            in_specs=[smem, smem] + [hbm] * 7 + [vmem] * 2,
            out_specs=vmem,
            scratch_shapes=[
                pltpu.VMEM((N, N), BF16),
                pltpu.VMEM((count, N), jnp.int32),
                pltpu.VMEM((2, count, N), BF16),
                pltpu.VMEM((KF, KF), F32),
                pltpu.VMEM((KF, KF), F32),
                pltpu.VMEM((N, LANES), BF16),
                pltpu.VMEM((LANES, N), BF16),
                pltpu.VMEM((2, count, LANES), BF16),
                pltpu.VMEM((2, LANES, count), BF16),
                pltpu.VMEM((ranks, 2, HALF, LANES), BF16),
                pltpu.VMEM((8, KF, LANES), BF16),
                pltpu.VMEM((KF, LANES), BF16),
                pltpu.VMEM((KF, LANES), BF16),
                pltpu.VMEM((LANES, LANES), BF16),
                pltpu.VMEM((LANES, LANES), BF16),
                pltpu.VMEM((LANES, LANES), BF16),
                pltpu.VMEM((LANES, N), BF16),
                pltpu.VMEM((LANES, GROUP * LANES), BF16),
                pltpu.VMEM((2, count, N), F32),
                pltpu.VMEM((CHUNKS, LANES, 2 * LANES), BF16),
                pltpu.VMEM((CHUNKS, 2 * LANES, LANES), BF16),
                pltpu.VMEM((2, CHUNKS, N, 2 * LANES), BF16),
                pltpu.VMEM((N, LANES), F32),
                pltpu.VMEM((KF, LANES), F32),
                pltpu.VMEM((count, LANES), F32),
                pltpu.VMEM((count, LANES), F32),
                pltpu.VMEM((count, LANES), F32),
                pltpu.SemaphoreType.DMA((12,)),
                pltpu.SemaphoreType.DMA((ranks,)),
                pltpu.SemaphoreType.DMA((ranks,)),
                pltpu.SemaphoreType.DMA((ranks,)),
                pltpu.SemaphoreType.DMA((ranks,)),
                pltpu.SemaphoreType.DMA((ranks,)),
                pltpu.SemaphoreType.DMA((ranks,)),
                pltpu.SemaphoreType.REGULAR((ranks,)),
                pltpu.SemaphoreType.DMA((2,)),
                pltpu.SemaphoreType.DMA((4,)),
                pltpu.SemaphoreType.DMA((4,)),
            ],
            compiler_params=pltpu.CompilerParams(collective_id=0, has_side_effects=True),
        )(
            orientation,
            eigen_weights.reshape(1, 1),
            mask,
            target,
            kernel_real,
            kernel_imag,
            jnp.asarray(mid),
            jnp.asarray(mid_t),
            jnp.asarray(rows_t),
            jnp.asarray(rim),
            jnp.asarray(rim_t),
        )

    in_specs = (
        P(None, "tile"),
        P("tile", None),
        P("kern", "tile"),
        P("kern", None, None),
        P("kern", None, None),
        P("kern"),
    )
    return jax.shard_map(
        per_device, mesh=mesh, in_specs=in_specs, out_specs=P("kern", "tile"), check_vma=False
    )
```

```python
import math

import jax
import jax.numpy as jnp
import ml_dtypes
import numpy as np
from jax import lax
from jax.experimental import pallas as pl
from jax.experimental.pallas import tpu as pltpu
from jax.sharding import PartitionSpec as P

N = 1152
HALO = 64
KF = 64
HALF = KF // 2
NE = 1280
LANES = 128
CHUNKS = N // LANES
GROUP = 2
BATCH = 4
AHEAD = 3
HELPED = 4

STEEPNESS = 4.0
THRESHOLD = 1.0
F32 = jnp.float32
BF16 = jnp.bfloat16
MESH = pl.DeviceIdType.MESH


def wave_pair():
    phase = np.mod(np.arange(NE)[:, None] * (np.arange(KF) - KF // 2)[None, :], NE).astype(np.float32)
    phase = phase * np.float32(2.0 * math.pi / NE)
    return np.concatenate([np.cos(phase), np.sin(phase)], 1).astype(ml_dtypes.bfloat16)


def tables(ranks):
    full = wave_pair()
    mid = full[HALO : HALO + N]
    right, left = full[HALO + N :], full[:HALO]
    rim = np.stack([np.concatenate([right, left]), np.concatenate([right[::-1], left[::-1]])])
    rows_t = np.transpose(mid.reshape(ranks, N // ranks, 2 * KF), (0, 2, 1))
    return mid, mid.T.copy(), rows_t.copy(), rim, np.transpose(rim, (0, 2, 1)).copy()


def dot(a, b):
    return jnp.dot(a, b, preferred_element_type=F32)


def body(
    ranks,
    orient,
    weight,
    mask_hbm,
    target_hbm,
    hr_hbm,
    hi_hbm,
    mid_hbm,
    mid_t_hbm,
    rows_t_hbm,
    rim_ref,
    rim_t_ref,
    out_ref,
    mask,
    target,
    wanted,
    hr,
    hi,
    mid,
    mid_t,
    rows,
    rows_t,
    spec_all,
    part_all,
    share,
    window,
    strip,
    halo_low,
    halo_high,
    columns,
    stacked,
    intensity,
    to_cols,
    from_cols,
    fields,
    partial,
    gradient,
    margin,
    margin_low,
    margin_high,
    local_sem,
    spec_send,
    spec_recv,
    cross_send,
    cross_recv,
    part_send,
    part_recv,
    here,
    target_sem,
    tile_send,
    tile_recv,
):
    tiles = lax.axis_size("tile")
    tile = lax.axis_index("tile")
    rank = lax.axis_index("kern")
    up = lax.rem(tile + 1, tiles)
    down = lax.rem(tile + tiles - 1, tiles)
    count = N // ranks

    def load(src, dst, slot):
        copy = pltpu.make_async_copy(src, dst, local_sem.at[slot])
        copy.start()
        return copy

    barrier = pltpu.get_barrier_semaphore()
    for other in range(1, ranks):

        @pl.when(other > rank)
        def _():
            pl.semaphore_signal(barrier, inc=1, device_id={"kern": other}, device_id_type=MESH)

    for other in (up, down):
        pl.semaphore_signal(barrier, inc=1, device_id={"tile": other}, device_id_type=MESH)

    get_hr = load(hr_hbm.at[0], hr, 0)
    get_hi = load(hi_hbm.at[0], hi, 1)
    get_mid_t = load(mid_t_hbm, mid_t, 2)
    get_first = load(mask_hbm.at[:, 0:LANES], mask.at[:, 0:LANES], 3)
    get_last = load(mask_hbm.at[:, N - LANES : N], mask.at[:, N - LANES : N], 4)
    get_inner = load(mask_hbm.at[:, LANES : N - LANES], mask.at[:, LANES : N - LANES], 5)
    get_mid = load(mid_hbm, mid, 6)
    get_target = load(target_hbm, target, 7)
    workers = ranks - HELPED
    whose = (rank, lax.rem(rank + workers, ranks))
    get_rows = [
        load(mid_hbm.at[pl.ds(pl.multiple_of(owner * count, 16), count)], rows.at[s], 8 + s)
        for s, owner in enumerate(whose)
    ]
    get_rows_t = [load(rows_t_hbm.at[owner], rows_t.at[s], 10 + s) for s, owner in enumerate(whose)]

    low = lax.broadcasted_iota(jnp.int32, (KF, 2 * KF), 1) < KF
    plus = jnp.where(low, 1.0, -1.0)
    minus = -plus

    def swap(x):
        return pltpu.roll(x, KF, 1)

    pl.semaphore_wait(barrier, rank + 2)

    for other in range(ranks - 1):

        @pl.when(jnp.logical_and(other < rank, jnp.logical_or(rank < workers, other >= workers)))
        def _():
            pl.semaphore_signal(here.at[rank], inc=1, device_id={"kern": other}, device_id_type=MESH)

    get_hr.wait()
    get_hi.wait()
    root = jnp.sqrt(jnp.full((KF, 2 * KF), weight[0, 0], F32))
    spectrum = (jnp.concatenate([hr[...], hi[...]], 1) * root).astype(BF16)
    spec_all[rank, 0] = spectrum[:HALF]
    spec_all[rank, 1] = spectrum[HALF:]
    core = lax.rem(tile, 2)

    def cross_copy(source):
        return pltpu.make_async_remote_copy(
            src_ref=spec_all.at[source, core],
            dst_ref=spec_all.at[source, core],
            send_sem=cross_send.at[source],
            recv_sem=cross_recv.at[source],
            device_id={"tile": tile + 1 - 2 * core},
            device_id_type=MESH,
        )

    def spec_copy(source, other):
        return pltpu.make_async_remote_copy(
            src_ref=spec_all.at[source, core],
            dst_ref=spec_all.at[source, core],
            send_sem=spec_send.at[other],
            recv_sem=spec_recv.at[source],
            device_id={"kern": other},
            device_id_type=MESH,
        )

    for other in sorted(range(workers), key=lambda o: abs(o - ranks // 2 + 1)):

        @pl.when(other < rank)
        def _():
            spec_copy(rank, other).start()

    def to_neighbours(src, dst_up, dst_down, first):
        copies = []
        for place, (dst, other) in enumerate(((dst_up, up), (dst_down, down))):
            copy = pltpu.make_async_remote_copy(
                src_ref=src,
                dst_ref=dst,
                send_sem=tile_send.at[first + place],
                recv_sem=tile_recv.at[first + place],
                device_id={"tile": other},
                device_id_type=MESH,
            )
            copy.start()
            copies.append(copy)
        return copies

    pairs = ranks // GROUP
    own = rank // GROUP
    ahead = pairs - own

    def turn(i):
        past = i - ahead
        return jnp.where(past < 0, own + i, own - 1 - past)

    def relay(at):
        for k in range(GROUP):
            other = at * GROUP + k

            @pl.when(other != rank)
            def _():
                spec_copy(other, rank).wait_recv()
                cross_copy(other).start()

    def answer(at):
        for k in range(GROUP):
            other = at * GROUP + k

            @pl.when(jnp.logical_and(other > rank, other < workers))
            def _():
                pl.semaphore_wait(here.at[other], 1)
                spec_copy(rank, other).start()

    get_mid_t.wait()
    get_first.wait()
    get_last.wait()
    first = dot(mid_t[...], mask[:, 0:LANES]).astype(BF16)
    last = dot(mid_t[...], mask[:, N - LANES : N]).astype(BF16)
    columns[:, 0:LANES] = first
    columns[:, N - LANES : N] = last
    edge = lax.broadcasted_iota(jnp.int32, (2 * KF, LANES), 1) < HALO
    strip[...] = jnp.where(edge, first.astype(F32), last.astype(F32)).astype(BF16)
    halo_copies = to_neighbours(strip, halo_low, halo_high, 0)

    get_inner.wait()
    for j in range(1, CHUNKS - 1):
        columns[:, j * LANES : (j + 1) * LANES] = dot(
            mid_t[...], mask[:, j * LANES : (j + 1) * LANES]
        ).astype(BF16)

    get_mid.wait()
    wide = lax.broadcasted_iota(jnp.int32, (LANES, 2 * KF), 1) < KF
    for j in range(CHUNKS):
        part = mid_t[:, j * LANES : (j + 1) * LANES]
        to_cols[j, 0:KF, 0:LANES] = part[:KF]
        to_cols[j, 0:KF, LANES:] = part[KF:]
        to_cols[j, KF:, 0:LANES] = -part[KF:]
        to_cols[j, KF:, LANES:] = part[:KF]
        block = mid[j * LANES : (j + 1) * LANES].astype(F32)
        from_cols[j, 0:LANES] = jnp.where(wide, block, -block).astype(BF16)
        from_cols[j, LANES:] = swap(block).astype(BF16)

    keep_right = orient[0, 1].astype(F32)
    keep_left = orient[0, 0].astype(F32)

    blocks = dot(columns[...], mid[...])
    upper = lax.broadcasted_iota(jnp.int32, (LANES, LANES), 0) < HALO
    keep = jnp.where(upper, keep_right, keep_left)
    rim = keep * rim_ref[0].astype(F32) + (1.0 - keep) * rim_ref[1].astype(F32)
    there = jnp.where(upper, jnp.where(tile < tiles - 1, 1.0, 0.0), jnp.where(tile > 0, 1.0, 0.0))
    rim = (rim * there).astype(BF16)
    for copy in halo_copies:
        copy.wait_recv()
    halo = jnp.where(edge, halo_high[...].astype(F32), halo_low[...].astype(F32)).astype(BF16)
    blocks = blocks + dot(halo, rim)
    lower = swap(blocks[KF:])
    spec = jnp.where(low, blocks[:KF] - lower, -(blocks[:KF] + lower)) * (1.0 / (NE * KF))
    spec_turned = swap(spec) * minus

    def kernel_parts(k):
        both = spec_all[k].reshape(KF, 2 * KF).astype(F32)
        other = swap(both)
        return jnp.where(low, both, other), jnp.where(low, other, both)

    for copy in [get_target] + get_rows + get_rows_t:
        copy.wait()
    wanted[0] = target[...].astype(F32).astype(BF16)
    target_copy = pltpu.make_async_remote_copy(
        src_ref=wanted.at[0],
        dst_ref=wanted.at[1],
        send_sem=target_sem.at[0],
        recv_sem=target_sem.at[1],
        device_id={"kern": lax.rem(rank + HELPED, ranks)},
        device_id_type=MESH,
    )

    @pl.when(rank >= workers)
    def _():
        for other in range(workers):
            spec_copy(rank, other).wait_send()
        target_copy.start()

    pair_rows = GROUP * count

    def forward(i, s):
        both = dot(rows[s], stacked[...]).astype(BF16)
        line = jnp.concatenate([both[:, k * LANES : (k + 1) * LANES] for k in range(GROUP)], 0)
        place = pl.ds(pl.multiple_of(i * pair_rows, 32), pair_rows)
        for j in range(CHUNKS):
            field = dot(line, to_cols[j])
            total = intensity[s, :, j * LANES : (j + 1) * LANES]
            for k in range(GROUP):
                one = field[k * count : (k + 1) * count]
                total = total + (one[:, :LANES] * one[:, :LANES] + one[:, LANES:] * one[:, LANES:])
            intensity[s, :, j * LANES : (j + 1) * LANES] = total
            fields[s, j, place] = field.astype(BF16)

    def arrive(i, carry):
        at = turn(i)
        answer(own + i + AHEAD)

        @pl.when(i + 1 < pairs)
        def _():
            relay(turn(i + 1))

        for k in range(GROUP):
            other = at * GROUP + k

            @pl.when(other != rank)
            def _():
                cross_copy(other).wait_recv()

            real, imag = kernel_parts(other)
            product = real * spec + imag * spec_turned
            stacked[0:KF, k * LANES : (k + 1) * LANES] = product.astype(BF16)
            stacked[KF:, k * LANES : (k + 1) * LANES] = (swap(product) * minus).astype(BF16)
        forward(i, 0)

        @pl.when(rank < HELPED)
        def _():
            forward(i, 1)

        return carry

    size = BATCH * count

    def adjoint(s):
        def chunk(j, carry):
            place = pl.ds(pl.multiple_of(j * LANES, LANES), LANES)
            total = intensity[s, :, place]
            resist = 1.0 / (1.0 + jnp.exp(-STEEPNESS * (total - THRESHOLD)))
            pattern = wanted[s, :, place].astype(F32)
            slope = (2.0 * (resist - pattern) * STEEPNESS * resist * (1.0 - resist)).astype(BF16)
            slope = jnp.concatenate([slope, slope], 1)
            slope = jnp.concatenate([slope] * BATCH, 0)
            for b in range(ranks // BATCH):
                weighted = fields[s, j, b * size : (b + 1) * size] * slope
                partial[b * size : (b + 1) * size] += dot(weighted, from_cols[j])
            return carry

        partial[...] = jnp.zeros_like(partial)
        lax.fori_loop(0, CHUNKS, chunk, 0)

        grad = jnp.zeros((KF, 2 * KF), F32)
        for k in range(0, ranks, 2):
            pair = [partial[(k + i) * count : (k + i + 1) * count].astype(BF16) for i in range(2)]
            wave = dot(rows_t[s], jnp.concatenate(pair, 1))
            for i in range(2):
                one = wave[:, i * LANES : (i + 1) * LANES]
                one = one[:KF] + swap(one[KF:]) * plus
                real, imag = kernel_parts(turn(k // GROUP) * GROUP + i)
                grad = grad + real * one + imag * (swap(one) * plus)
        gradient[...] += grad * (2.0 / (NE * KF))

    gradient[...] = jnp.zeros_like(gradient)

    @pl.when(rank < workers)
    def _():
        intensity[...] = jnp.zeros_like(intensity)
        for i in range(AHEAD):
            answer(own + i)
        relay(own)
        lax.fori_loop(0, pairs, arrive, 0)
        adjoint(0)

    @pl.when(rank < HELPED)
    def _():
        target_copy.wait_recv()
        adjoint(1)

    def ring_copy(src, slot, turn_by, flip):
        to = lax.rem(own + turn_by, pairs) * GROUP + (lax.rem(rank, GROUP) if not flip else 1 - lax.rem(rank, GROUP))
        copy = pltpu.make_async_remote_copy(
            src_ref=src,
            dst_ref=part_all.at[slot],
            send_sem=part_send.at[slot],
            recv_sem=part_recv.at[slot],
            device_id={"kern": to},
            device_id_type=MESH,
        )
        copy.start()
        return copy

    for other in range(workers + 1, ranks):

        @pl.when(jnp.logical_and(rank >= workers, other > rank))
        def _():
            pl.semaphore_wait(here.at[other], 1)

    share[...] = gradient[...].astype(BF16)
    near = [
        ring_copy(share, slot, turn_by, flip)
        for slot, (turn_by, flip) in enumerate(
            ((pairs - 1, False), (pairs - 1, True), (1, False), (1, True), (0, True))
        )
    ]
    total = share[...].astype(F32)
    for slot, copy in enumerate(near):
        copy.wait_recv()
        total = total + part_all[slot].astype(F32)
    window[...] = total.astype(BF16)
    far = [
        ring_copy(window, len(near) + slot, turn_by, False)
        for slot, turn_by in enumerate((pairs // 2, pairs // 4, pairs - pairs // 4))
    ]
    for slot, copy in enumerate(far):
        copy.wait_recv()
        total = total + part_all[len(near) + slot].astype(F32)
    grad = total.astype(BF16).astype(F32)
    both = jnp.concatenate([grad, swap(grad) * minus], 0).astype(BF16)
    line = dot(rows[0], both)
    side = lax.broadcasted_iota(jnp.int32, (count, 2 * KF), 1) < KF
    line = jnp.where(side, line, -line).astype(BF16)
    first_lanes = lax.broadcasted_iota(jnp.int32, (LANES, LANES), 1) < HALO
    keep = jnp.where(first_lanes, keep_right, keep_left)
    rim = keep * rim_t_ref[0].astype(F32) + (1.0 - keep) * rim_t_ref[1].astype(F32)
    margin[...] = dot(line, rim.astype(BF16))
    margin_copies = to_neighbours(margin, margin_low, margin_high, 2)
    out_ref[...] = dot(line, mid_t[...])
    for copy in margin_copies:
        copy.wait_recv()
    out_ref[:, 0:LANES] += jnp.where(jnp.logical_and(side, tile > 0), margin_low[...], 0.0)
    out_ref[:, N - LANES : N] += jnp.where(
        jnp.logical_and(jnp.logical_not(side), tile < tiles - 1), margin_high[...], 0.0
    )
    for copy in halo_copies + near + far + margin_copies:
        copy.wait_send()

    @pl.when(rank >= workers)
    def _():
        target_copy.wait_send()

    for other in range(workers):

        @pl.when(jnp.logical_and(other != rank, rank < workers))
        def _():
            spec_copy(rank, other).wait_send()

    for other in range(ranks):

        @pl.when(jnp.logical_and(other != rank, rank < workers))
        def _():
            cross_copy(other).wait_send()


def solution(mesh):
    ranks = mesh.shape["kern"]
    count = N // ranks
    mid, mid_t, rows_t, rim, rim_t = tables(ranks)

    def per_device(mask, orientation, target, kernel_real, kernel_imag, eigen_weights):
        hbm = pl.BlockSpec(memory_space=pl.ANY)
        vmem = pl.BlockSpec(memory_space=pltpu.VMEM)
        smem = pl.BlockSpec(memory_space=pltpu.SMEM)
        return pl.pallas_call(
            lambda *refs: body(ranks, *refs),
            out_shape=jax.ShapeDtypeStruct((count, N), F32),
            in_specs=[smem, smem] + [hbm] * 7 + [vmem] * 2,
            out_specs=vmem,
            scratch_shapes=[
                pltpu.VMEM((N, N), BF16),
                pltpu.VMEM((count, N), jnp.int32),
                pltpu.VMEM((2, count, N), BF16),
                pltpu.VMEM((KF, KF), F32),
                pltpu.VMEM((KF, KF), F32),
                pltpu.VMEM((N, LANES), BF16),
                pltpu.VMEM((LANES, N), BF16),
                pltpu.VMEM((2, count, LANES), BF16),
                pltpu.VMEM((2, LANES, count), BF16),
                pltpu.VMEM((ranks, 2, HALF, LANES), BF16),
                pltpu.VMEM((8, KF, LANES), BF16),
                pltpu.VMEM((KF, LANES), BF16),
                pltpu.VMEM((KF, LANES), BF16),
                pltpu.VMEM((LANES, LANES), BF16),
                pltpu.VMEM((LANES, LANES), BF16),
                pltpu.VMEM((LANES, LANES), BF16),
                pltpu.VMEM((LANES, N), BF16),
                pltpu.VMEM((LANES, GROUP * LANES), BF16),
                pltpu.VMEM((2, count, N), F32),
                pltpu.VMEM((CHUNKS, LANES, 2 * LANES), BF16),
                pltpu.VMEM((CHUNKS, 2 * LANES, LANES), BF16),
                pltpu.VMEM((2, CHUNKS, N, 2 * LANES), BF16),
                pltpu.VMEM((N, LANES), F32),
                pltpu.VMEM((KF, LANES), F32),
                pltpu.VMEM((count, LANES), F32),
                pltpu.VMEM((count, LANES), F32),
                pltpu.VMEM((count, LANES), F32),
                pltpu.SemaphoreType.DMA((12,)),
                pltpu.SemaphoreType.DMA((ranks,)),
                pltpu.SemaphoreType.DMA((ranks,)),
                pltpu.SemaphoreType.DMA((ranks,)),
                pltpu.SemaphoreType.DMA((ranks,)),
                pltpu.SemaphoreType.DMA((ranks,)),
                pltpu.SemaphoreType.DMA((ranks,)),
                pltpu.SemaphoreType.REGULAR((ranks,)),
                pltpu.SemaphoreType.DMA((2,)),
                pltpu.SemaphoreType.DMA((4,)),
                pltpu.SemaphoreType.DMA((4,)),
            ],
            compiler_params=pltpu.CompilerParams(collective_id=0, has_side_effects=True),
        )(
            orientation,
            eigen_weights.reshape(1, 1),
            mask,
            target,
            kernel_real,
            kernel_imag,
            jnp.asarray(mid),
            jnp.asarray(mid_t),
            jnp.asarray(rows_t),
            jnp.asarray(rim),
            jnp.asarray(rim_t),
        )

    in_specs = (
        P(None, "tile"),
        P("tile", None),
        P("kern", "tile"),
        P("kern", None, None),
        P("kern", None, None),
        P("kern"),
    )
    return jax.shard_map(
        per_device, mesh=mesh, in_specs=in_specs, out_specs=P("kern", "tile"), check_vma=False
    )
```
